32 devices in a mesh: group: 2 (over y), gx: 4 (over z), gy: 2 (over x), gz: 2 (over core).
Axes of the slice: x: 2, y: 2, z: 4, core: 2. Of those that a mesh axis runs over, the one named last changes fastest.
Arguments:
- tokens: bfloat16 [12, 8192], P('group', 'gx'), parts along dimension 0, may hold values from -40 to 40
- norm_gain: float32 [8192], P('gx'), may hold values from 0.1 to 1.9
- q_weight: bfloat16 [8192, 4096], P('gx', ('gy', 'gz')), may hold values from -0.0625 to 0.0625
- kv_weight: bfloat16 [8192, 512], P('gx'), may hold values from -0.0625 to 0.0625
- out_weight: bfloat16 [4096, 8192], P(('gy', 'gz'), 'gx'), may hold values from -0.09375 to 0.09375
- gate_weight: bfloat16 [8192, 16384], P('gx', ('gy', 'gz')), may hold values from -0.0625 to 0.0625
- up_weight: bfloat16 [8192, 16384], P('gx', ('gy', 'gz')), may hold values from -0.0625 to 0.0625
- down_weight: bfloat16 [16384, 8192], P(('gy', 'gz'), 'gx'), may hold values from -0.046875 to 0.046875
- kv_cache: bfloat16 [12, 2048, 512], P(('group', 'gy'), ('gx', 'gz')), parts along dimension 0, may hold values from -55 to 55
- lengths: int32 [12], P(('group', 'gy')), parts along dimension 0, may hold values from 1026 to 2048, as said below
Outputs:
- mixed: bfloat16 [12, 8192], P('group', 'gx'), parts along dimension 0
- new_kv: bfloat16 [12, 512], P(('group', 'gy')), parts along dimension 0
The draws below stay inside these ranges and needn't reach their ends.
There are 2 independent parts, one for each index of `group`. The reference program is written for one: setup_inputs(seed, part) draws one part's arguments, and reference() takes and returns one part's arrays. A program takes and returns all parts, laid end to end along the dimension named above; an argument that names none is the same for every part. Nothing has to cross between parts.
Inputs may be any that keep to these rules, and one draw needn't show every extreme that they name: The new token of sequence s stands at position lengths[s]; cache positions from lengths[s] on hold no valid token; some sequence has all 2048 positions valid.
All inputs are finite; a program needn't handle non-finite values.
Results may differ from the reference program's by a relative error of at most 0.012.
Values may be sent and summed in bfloat16 or wider, within the bound.
A program may use at most 128 MiB of HBM per device.

```python
import jax
import jax.numpy as jnp
from jax import lax

D = 8192
FF = 16384
HEADS = 16
HEAD_DIM = 256
SEQS = 6
CTX = 2048


def draw_tokens(key, part):
    first_key, second_key = jax.random.split(jax.random.fold_in(key, 11), 2)
    place = jnp.arange(D, dtype=jnp.float32) / D
    rough = jax.random.uniform(second_key, (D,), jnp.float32, 0.5, 1.5)
    noise = jax.random.normal(first_key, (SEQS, D), jnp.float32)
    col_scales = 3.0 ** (place - 0.5) * rough
    values = jnp.clip(noise, -4.0, 4.0) * col_scales[None, :]
    return jnp.clip(values, -40.0, 40.0).astype(jnp.bfloat16)


def draw_lengths(key, part):
    first_key, second_key = jax.random.split(jax.random.fold_in(key, 37), 2)
    drawn = jax.random.randint(first_key, (SEQS,), CTX // 2 + 2, CTX + 1)
    full_row = jax.random.randint(second_key, (), 0, SEQS)
    rows = jnp.arange(SEQS, dtype=jnp.int32)
    return jnp.where(rows == full_row, CTX, drawn).astype(jnp.int32)


def draw_kv_cache(key, part):
    first_key = jax.random.fold_in(jax.random.fold_in(key, 23), 0)
    second_key = jax.random.fold_in(jax.random.fold_in(key, 23), 1)
    fourth_key = jax.random.fold_in(jax.random.fold_in(key, 23), 3)
    fifth_key = jax.random.fold_in(jax.random.fold_in(key, 23), 4)
    keys = 2.5 * jnp.clip(jax.random.normal(first_key, (SEQS, CTX, HEAD_DIM), jnp.float32), -4.0, 4.0)
    values = 1.5 * jnp.clip(jax.random.normal(second_key, (SEQS, CTX, HEAD_DIM), jnp.float32), -4.0, 4.0)
    strength = jax.random.uniform(fourth_key, (SEQS, 1, 1), jnp.float32, 30.0, 45.0)
    signs = jax.random.randint(fifth_key, (SEQS, 1, HEAD_DIM), 0, 2).astype(jnp.float32) * 2.0 - 1.0
    factors = jnp.array([1.0, 1.02], jnp.float32)[None, :, None]
    strong = strength * signs * factors
    half = CTX // 2
    keys = jnp.concatenate([keys[:, :half, :], strong, keys[:, half + 2:, :]], 1)
    return jnp.concatenate([keys, values], 2).astype(jnp.bfloat16)


def block_levels(key, dims, cuts, low, largest):
    level = 1.0
    for position, shards_of in cuts:
        heights = jax.random.uniform(jax.random.fold_in(jax.random.fold_in(key, 6), position), (shards_of,), jnp.float32, low / len(cuts), largest / len(cuts))
        level = level * jnp.repeat(jnp.exp(heights), dims[position] // shards_of).reshape((-1,) + (1,) * (len(dims) - 1 - position))
    return level


def centred(key, extent, scale, most, pieces=(), held_as=jnp.bfloat16):
    values = scale * jax.random.normal(key, extent, jnp.float32)
    if pieces:
        values = values * block_levels(key, extent, pieces, -0.22, 0.18)
    return jnp.clip(values, -most, most).astype(held_as)


def setup_inputs(seed: int = 0, part: int = 0) -> dict:
    streams_of = jax.random.split(jax.random.key(seed), 11)
    part_keys = jax.random.split(jax.random.fold_in(streams_of[10], part), 11)
    tokens = draw_tokens(jax.random.fold_in(jax.random.fold_in(streams_of[10], part), 71), part)
    norm_gain = jnp.clip(1.0 + 0.18 * jax.random.normal(streams_of[1], (D,), jnp.float32), 0.1, 1.9)
    q_weight = centred(streams_of[2], (D, HEADS * HEAD_DIM), D ** -0.5, 0.0625, ((0, 4), (1, 4)))
    kv_weight = centred(streams_of[3], (D, 2 * HEAD_DIM), D ** -0.5, 0.0625, ((0, 4),))
    out_weight = centred(streams_of[4], (HEADS * HEAD_DIM, D), (HEADS * HEAD_DIM) ** -0.5, 0.09375, ((0, 4), (1, 4)))
    gate_weight = centred(streams_of[5], (D, FF), D ** -0.5, 0.0625, ((0, 4), (1, 4)))
    up_weight = centred(streams_of[6], (D, FF), D ** -0.5, 0.0625, ((0, 4), (1, 4)))
    down_weight = centred(streams_of[7], (FF, D), FF ** -0.5, 0.046875, ((0, 4), (1, 4)))
    kv_cache = draw_kv_cache(jax.random.fold_in(jax.random.fold_in(streams_of[10], part), 71), part)
    lengths = draw_lengths(jax.random.fold_in(jax.random.fold_in(streams_of[10], part), 71), part)
    return {"tokens": tokens, "norm_gain": norm_gain, "q_weight": q_weight, "kv_weight": kv_weight, "out_weight": out_weight, "gate_weight": gate_weight, "up_weight": up_weight, "down_weight": down_weight, "kv_cache": kv_cache, "lengths": lengths}


epsilon = 1e-05
masked_fill = -1e+30
rotary_base = 10000.0

def rotate(values, angle):
    middle = values.shape[-1] // 2
    first = values[..., :middle]
    second = values[..., middle:]
    cosine = jnp.cos(angle)
    sine_part = jnp.sin(angle)
    return jnp.concatenate([first * cosine - second * sine_part, first * sine_part + second * cosine], -1)

def angles(lengths, head_dim):
    middle = head_dim // 2
    spread = rotary_base ** (-jnp.arange(middle, dtype=jnp.float32) / middle)
    return lengths.astype(jnp.float32)[:, None] * spread[None, :]

def reference(tokens, norm_gain, q_weight, kv_weight, out_weight, gate_weight, up_weight, down_weight, kv_cache, lengths):
    inputs = tokens.astype(jnp.float32)
    center = lax.optimization_barrier(jnp.sum(inputs, 1)) / D
    spread_sq = lax.optimization_barrier(jnp.sum(inputs * inputs, 1)) / D - center * center
    normed = ((inputs - center[:, None]) * lax.rsqrt(spread_sq + epsilon)[:, None] * norm_gain[None, :]).astype(jnp.bfloat16)
    query = jnp.dot(normed, q_weight, preferred_element_type=jnp.float32).astype(jnp.bfloat16)
    keyval = jnp.dot(normed, kv_weight, preferred_element_type=jnp.float32)
    gate = jnp.dot(normed, gate_weight, preferred_element_type=jnp.float32)
    upward = jnp.dot(normed, up_weight, preferred_element_type=jnp.float32)
    hidden = (jax.nn.silu(gate) * upward).astype(jnp.bfloat16)
    angle = angles(lengths, HEAD_DIM)
    new_kv = jnp.concatenate([rotate(keyval[:, :HEAD_DIM], angle), keyval[:, HEAD_DIM:]], 1).astype(jnp.bfloat16)
    rotated = rotate(query.astype(jnp.float32).reshape(SEQS, HEADS, HEAD_DIM), angle[:, None, :]).astype(jnp.bfloat16)
    scale = HEAD_DIM ** (-0.5)
    positions = jnp.arange(CTX, dtype=jnp.int32)

    def one_sequence(packed):
        queries, cache, length, key_new, value_new = packed
        scores = jnp.dot(queries, cache[:, :HEAD_DIM].T, preferred_element_type=jnp.float32) * scale
        own_score = jnp.dot(queries, key_new, preferred_element_type=jnp.float32) * scale
        live = positions < length
        hidden_scores = jnp.where(live[None, :], scores, masked_fill)
        top = jnp.maximum(lax.optimization_barrier(jnp.max(hidden_scores, 1)), own_score)
        weights = jnp.where(live[None, :], jnp.exp(hidden_scores - top[:, None]), 0.0)
        numer = jnp.dot(weights.astype(jnp.bfloat16), cache[:, HEAD_DIM:], preferred_element_type=jnp.float32)
        denom = lax.optimization_barrier(jnp.sum(weights, 1))
        own_weight = jnp.exp(own_score - top)
        numer = numer + own_weight[:, None] * value_new.astype(jnp.float32)[None, :]
        denom = denom + own_weight
        return (numer / denom[:, None]).astype(jnp.bfloat16)
    attended = lax.map(one_sequence, (rotated, kv_cache, lengths, new_kv[:, :HEAD_DIM], new_kv[:, HEAD_DIM:]))
    attended = attended.reshape(SEQS, HEADS * HEAD_DIM)
    total = jnp.dot(attended, out_weight, preferred_element_type=jnp.float32) + jnp.dot(hidden, down_weight, preferred_element_type=jnp.float32)
    mixed = (inputs + total).astype(jnp.bfloat16)
    return (mixed, new_kv)
```

```python
import functools
import itertools

import jax
import jax.numpy as jnp
import numpy as np
from jax import lax
from jax.experimental import pallas as pl
from jax.experimental.pallas import tpu as pltpu
from jax.sharding import PartitionSpec as P

D = 8192
HEADS = 16
HEAD_DIM = 256


epsilon = 1e-05
masked_fill = -1e30
rotary_base = 10000.0


def joined(part, axis, combine):
    gathered = jax.tree.map(lambda a: lax.all_gather(a, axis), part)

    def take(source):
        return jax.tree.map(lambda a: lax.dynamic_index_in_dim(a, source, 0, False), gathered)

    return lax.fori_loop(
        1, lax.axis_size(axis), lambda source, state: combine(state, take(source)), take(0)
    )


def rotate(values, angle):
    middle = values.shape[-1] // 2
    first = values[..., :middle]
    second = values[..., middle:]
    cosine = jnp.cos(angle)
    sine_part = jnp.sin(angle)
    return jnp.concatenate(
        [first * cosine - second * sine_part, first * sine_part + second * cosine], -1
    )


def angles(lengths, head_dim):
    middle = head_dim // 2
    spread = rotary_base ** (-jnp.arange(middle, dtype=jnp.float32) / middle)
    return lengths.astype(jnp.float32)[:, None] * spread[None, :]


def combine(earlier, later):
    top = jnp.maximum(earlier[0], later[0])
    first_scale = jnp.exp(earlier[0] - top)
    second_scale = jnp.exp(later[0] - top)
    numer = earlier[1] * first_scale[..., None] + later[1] * second_scale[..., None]
    denom = earlier[2] * first_scale + later[2] * second_scale
    return (top, numer, denom)


def body(
    tokens,
    norm_gain,
    q_weight,
    kv_weight,
    out_weight,
    gate_weight,
    up_weight,
    down_weight,
    kv_cache,
    lengths,
):
    inputs = tokens.astype(jnp.float32)
    totals = lax.psum((jnp.sum(inputs, 1), jnp.sum(inputs * inputs, 1)), "gx")
    center = totals[0] / D
    spread_sq = totals[1] / D - center * center
    normed = (
        (inputs - center[:, None]) * lax.rsqrt(spread_sq + epsilon)[:, None] * norm_gain[None, :]
    ).astype(jnp.bfloat16)
    query_part = jnp.dot(normed, q_weight, preferred_element_type=jnp.float32)
    keyval_part = jnp.dot(normed, kv_weight, preferred_element_type=jnp.float32)
    gate_part = jnp.dot(normed, gate_weight, preferred_element_type=jnp.float32)
    up_part = jnp.dot(normed, up_weight, preferred_element_type=jnp.float32)
    query, keyval, gate, upward = lax.psum((query_part, keyval_part, gate_part, up_part), "gx")
    hidden = (jax.nn.silu(gate) * upward).astype(jnp.bfloat16)
    seq_dev = lengths.shape[0]
    row_groups = lax.axis_size("gy")
    block = q_weight.shape[1]
    first_row = lax.axis_index("gy") * seq_dev
    angle = angles(lengths, HEAD_DIM)
    own_keyval = lax.dynamic_slice_in_dim(keyval, first_row, seq_dev, 0)
    new_kv = jnp.concatenate(
        [rotate(own_keyval[:, :HEAD_DIM], angle), own_keyval[:, HEAD_DIM:]], 1
    ).astype(jnp.bfloat16)
    query_bf = query.astype(jnp.bfloat16)
    every_head = lax.all_gather(query_bf, ("gy", "gz"), axis=1, tiled=True)
    own_query = lax.dynamic_slice_in_dim(every_head, first_row, seq_dev, 0)
    rotated = rotate(
        own_query.astype(jnp.float32).reshape(seq_dev, HEADS, HEAD_DIM), angle[:, None, :]
    ).astype(jnp.bfloat16)
    ctx_dev = kv_cache.shape[1]
    offset = lax.axis_index(("gx", "gz")) * ctx_dev
    positions = offset + jnp.arange(ctx_dev, dtype=jnp.int32)
    live = positions[None, :] < lengths[:, None]
    scale = HEAD_DIM ** (-0.5)
    scores = (
        jnp.einsum(
            "shd,scd->shc", rotated, kv_cache[:, :, :HEAD_DIM], preferred_element_type=jnp.float32
        )
        * scale
    )
    key_new = new_kv[:, :HEAD_DIM]
    value_new = new_kv[:, HEAD_DIM:]
    own_score = (
        jnp.einsum("shd,sd->sh", rotated, key_new, preferred_element_type=jnp.float32) * scale
    )
    hidden_scores = jnp.where(live[:, None, :], scores, masked_fill)
    local_top = jnp.maximum(jnp.max(hidden_scores, 2), own_score)
    weights = jnp.where(live[:, None, :], jnp.exp(hidden_scores - local_top[..., None]), 0.0)
    numer = jnp.einsum(
        "shc,scd->shd",
        weights.astype(jnp.bfloat16),
        kv_cache[:, :, HEAD_DIM:],
        preferred_element_type=jnp.float32,
    )
    denom = jnp.sum(weights, 2)
    top, numer, denom = joined((local_top, numer, denom), ("gx", "gz"), combine)
    own_weight = jnp.exp(own_score - top)
    numer = numer + own_weight[..., None] * value_new.astype(jnp.float32)[:, None, :]
    denom = denom + own_weight
    attended = (numer / denom[..., None]).astype(jnp.bfloat16)
    grouped = attended.reshape(seq_dev, row_groups, HEADS * HEAD_DIM // row_groups)
    picked = lax.dynamic_slice_in_dim(grouped, lax.axis_index("gz") * block, block, 2)
    head_block = lax.all_to_all(picked, "gy", split_axis=1, concat_axis=0, tiled=True).reshape(
        seq_dev * row_groups, block
    )
    partial_value = jnp.dot(head_block, out_weight, preferred_element_type=jnp.float32) + jnp.dot(
        hidden, down_weight, preferred_element_type=jnp.float32
    )
    total = lax.psum(partial_value, ("gy", "gz"))
    mixed = (inputs + total).astype(jnp.bfloat16)
    return (mixed, new_kv)


MESH = pl.DeviceIdType.MESH
F32 = jnp.float32
BF16 = jnp.bfloat16


def kernel(
    dims,
    lengths_h,
    tokens_h,
    gain_h,
    spread_h,
    q_h,
    kv_h,
    cache_h,
    gate_h,
    up_h,
    out_h,
    down_h,
    mixed_ref,
    newkv_ref,
    lengths_ref,
    tokens_v,
    gain_v,
    spread_v,
    q_v,
    kv_v,
    cache_v,
    gu_v,
    out_v,
    down_v,
    load_sem,
    gu_sem,
    down_sem,
    x_v,
    normed_v,
    s1_v,
    r1_v,
    kvs_v,
    kvq_v,
    qsend_v,
    qall_v,
    rot_v,
    part_v,
    prs_v,
    gsend_v,
    grs_v,
    own_v,
    hid_v,
    acc_v,
    heads_v,
    fin_v,
    send_sem,
    recv_sem,
    h_recv,
    f_recv,
):
    ngx, ngy, ngz, rows, rp = dims
    gx, gy, gz = lax.axis_index("gx"), lax.axis_index("gy"), lax.axis_index("gz")
    dx = x_v.shape[1]
    qd = q_v.shape[1]
    heads_dev = qd // HEAD_DIM
    own_heads = heads_dev // ngx
    qo = own_heads * HEAD_DIM
    kw = kv_v.shape[1]
    seq_dev = cache_v.shape[0]
    ctx_dev = cache_v.shape[1]
    fb = gu_v.shape[3]
    owners = ngx * ngz
    spots = ngy * ngz
    pairs = HEADS // 2
    pairs_dev = heads_dev // 2
    slots = rp // 2
    wide = 16 // pairs_dev
    scale = HEAD_DIM ** (-0.5)
    middle = HEAD_DIM // 2
    half = dx // 2
    me_owner = gx * ngz + gz
    spot = gy * ngz + gz

    def rolled(values, shift, axis):
        shift = shift % values.shape[axis]
        return pltpu.roll(values, shift, axis) if shift else values

    def other(j):
        return jnp.where(gx <= j, j + 1, j)

    def block_at(step):
        return gx if step == ngx - 1 else other(step)

    def source_at(step):
        return gx if step == 0 else other(step - 1)

    def columns_of(block, width):
        return pl.ds(pl.multiple_of(block * width, width), width)

    loads = [
        pltpu.make_async_copy(a, b, load_sem.at[i])
        for i, (a, b) in enumerate(
            (
                (tokens_h, tokens_v),
                (gain_h, gain_v),
                (spread_h, spread_v),
                (kv_h.at[:, columns_of(spot, kw)], kv_v),
                (q_h, q_v),
                (cache_h, cache_v),
                (out_h, out_v),
                (lengths_h, lengths_ref),
            )
        )
    ]

    def gu_start(step):
        columns = columns_of(block_at(step), fb)
        pltpu.make_async_copy(gate_h.at[:, columns], gu_v.at[step, 0], gu_sem.at[step]).start()
        pltpu.make_async_copy(up_h.at[:, columns], gu_v.at[step, 1], gu_sem.at[step]).start()

    def down_copy(step):
        picked = columns_of(source_at(step), fb)
        return pltpu.make_async_copy(down_h.at[picked], down_v.at[step], down_sem.at[step])

    offsets = [o for o in itertools.product(range(ngx), range(ngy), range(ngz)) if any(o)]

    def shifted(ox, oy, oz):
        return lax.rem(gx + ox, ngx), lax.rem(gy + oy, ngy), lax.rem(gz + oz, ngz)

    def at(px, py, pz):
        return {"gx": px, "gy": py, "gz": pz}

    barrier = pltpu.get_barrier_semaphore()
    for offset in offsets:
        pl.semaphore_signal(barrier, inc=1, device_id=at(*shifted(*offset)), device_id_type=MESH)

    for i in (0, 1, 2, 7, 3, 4):
        loads[i].start()

    sc0 = jax.named_scope('begin')
    sc0.__enter__()
    loads[0].wait()
    gu_start(0)
    x_v[...] = jnp.zeros_like(x_v)
    x_v[0:rows, :] = tokens_v[...].astype(F32)
    x = x_v[...]
    lane = lax.broadcasted_iota(jnp.int32, (rp, 128), 1)
    sums = jnp.sum(x, 1, keepdims=True)
    stat = jnp.where(lane < 64, sums, jnp.sum(x * x, 1, keepdims=True))
    loads[1].wait()
    gu_start(1)
    spare = lax.broadcasted_iota(jnp.int32, (rp, dx), 0) == rows
    centred = jnp.where(spare, 1.0, x - sums / dx)
    normed_v[...] = (centred * gain_v[...]).astype(BF16)

    loads[2].wait()
    loads[7].wait()
    loads[5].start()
    line = lax.rem(lax.broadcasted_iota(jnp.int32, (rp, middle), 0), slots)
    length = jnp.zeros((rp, middle), jnp.int32)
    for s in range(seq_dev):
        length = jnp.where(line == s, lengths_ref[s], length)
    angle = length.astype(F32) * spread_v[...]
    cosine = jnp.cos(angle)
    sine = jnp.sin(angle)

    sc0.__exit__(None, None, None)
    sc0 = jax.named_scope('qdot')
    sc0.__enter__()
    loads[3].wait()
    gu_start(2)
    kv_part = jnp.dot(normed_v[...], kv_v[...], preferred_element_type=F32)
    loads[4].wait()
    for step in range(3, ngx):
        gu_start(step)
    q_part = jnp.dot(normed_v[...], q_v[...], preferred_element_type=F32)
    for j in range(ngx):
        s1_v[j, :, :qo] = q_part[:, j * qo : (j + 1) * qo]
        s1_v[j, :, qo : qo + kw] = kv_part
        s1_v[j, :, qo + kw :] = stat

    sc0.__exit__(None, None, None)
    with jax.named_scope('barrier'):
        pl.semaphore_wait(barrier, len(offsets))

    def send(source, target, sends, receives, device):
        pltpu.make_async_remote_copy(
            src_ref=source,
            dst_ref=target,
            send_sem=sends,
            recv_sem=receives,
            device_id=device,
            device_id_type=MESH,
        ).start()

    def arrival(slot, semaphore):
        return pltpu.make_async_remote_copy(
            src_ref=slot,
            dst_ref=slot,
            send_sem=semaphore,
            recv_sem=semaphore,
            device_id=at(gx, gy, gz),
            device_id_type=MESH,
        )

    def arrived(slot, semaphore):
        arrival(slot, semaphore).wait_recv()

    def left(slot, semaphore):
        arrival(slot, semaphore).wait_send()

    for k in range(1, ngx):
        peer = lax.rem(gx + k, ngx)
        send(s1_v.at[peer], r1_v.at[gx], send_sem.at[0], recv_sem.at[0], at(peer, gy, gz))
    r1_v[gx] = s1_v[gx]

    def gate_up(step):
        pltpu.make_async_copy(gu_v.at[step], gu_v.at[step], gu_sem.at[step]).wait()
        if step == 0:
            down_copy(0).start()
            down_copy(1).start()
        elif step == 1:
            for later in range(2, ngx - 1):
                down_copy(later).start()
            loads[6].start()
        elif step == 2:
            down_copy(ngx - 1).start()
        for which in range(2):
            part = jnp.dot(normed_v[...], gu_v[step, which], preferred_element_type=F32)
            if step < ngx - 1:
                gsend_v[step, which] = part.astype(BF16)
            else:
                own_v[which] = part
        if step < ngx - 1:
            send(
                gsend_v.at[step],
                grs_v.at[gx],
                send_sem.at[1],
                recv_sem.at[1],
                at(block_at(step), gy, gz),
            )

    def moments():
        arrived(r1_v.at[pl.ds(0, ngx - 1)], recv_sem.at[0])
        totals = r1_v[0, :, qo + kw :]
        for k in range(1, ngx):
            totals = totals + r1_v[k, :, qo + kw :]
        center = totals[:, 0:1] / D
        spread_sq = totals[:, 64:65] / D - center * center
        drift = [r1_v[k, :, qo + kw : qo + kw + 1] / dx - center for k in range(ngx)]
        return drift, lax.rsqrt(spread_sq + epsilon)

    rowid = lax.broadcasted_iota(jnp.int32, (rp, HEAD_DIM), 0)

    def packed(values, y):
        upper = rolled(values, -y * seq_dev, 0)
        lower = rolled(values, slots - y * seq_dev, 0)
        keep = lax.broadcasted_iota(jnp.int32, values.shape, 0) < slots
        return jnp.where(keep, upper, lower)

    def gather_query():
        total = None
        for k in range(ngx):
            values = r1_v[k, :, : qo + kw]
            part = values + drift[k] * values[rows : rows + 1, :]
            total = part if total is None else total + part
        total = total * inverse
        mine = spot * heads_dev + gx * own_heads
        for y in range(ngy):
            for h in range(own_heads):
                piece = total[:, h * HEAD_DIM : (h + 1) * HEAD_DIM]
                qsend_v[y, h] = packed(piece, y).astype(BF16)
            kvs_v[y] = packed(total[:, qo:], y)
        for offset in offsets:
            px, py, pz = shifted(*offset)
            send(
                qsend_v.at[py],
                qall_v.at[pl.ds(mine, own_heads)],
                send_sem.at[2],
                recv_sem.at[2],
                at(px, py, pz),
            )
            if not offset[0]:
                send(kvs_v.at[py], kvq_v.at[spot], send_sem.at[3], recv_sem.at[3], at(px, py, pz))
        for h in range(own_heads):
            qall_v[mine + h] = qsend_v[gy, h]
        kvq_v[spot] = kvs_v[gy]

    def attend():
        arrived(kvq_v.at[pl.ds(0, spots - 1)], recv_sem.at[3])
        keyval = jnp.concatenate([kvq_v[k] for k in range(spots)], 1)
        a = keyval[:, :middle]
        b = keyval[:, middle:HEAD_DIM]
        newkv = jnp.concatenate(
            [a * cosine - b * sine, a * sine + b * cosine, keyval[:, HEAD_DIM:]], 1
        ).astype(BF16)
        newkv_ref[...] = newkv[:seq_dev]
        newkv = newkv.astype(F32)
        arrived(qall_v.at[pl.ds(0, HEADS - own_heads)], recv_sem.at[2])
        owns = []
        for p in range(pairs):
            q = jnp.where(rowid < slots, qall_v[2 * p].astype(F32), qall_v[2 * p + 1].astype(F32))
            a = q[:, :middle]
            b = q[:, middle:]
            first = (a * cosine - b * sine).astype(BF16).astype(F32)
            second = (a * sine + b * cosine).astype(BF16).astype(F32)
            rot_v[p, :, :middle] = first
            rot_v[p, :, middle:] = second
            product = first * newkv[:, :middle] + second * newkv[:, middle:HEAD_DIM]
            owns.append(jnp.sum(product, 1, keepdims=True) * scale)
        count = pairs * rp
        rotated = rot_v[...].reshape(count, HEAD_DIM).astype(BF16)
        own = jnp.where(me_owner == 0, jnp.concatenate(owns, 0), masked_fill)
        line = lax.rem(lax.broadcasted_iota(jnp.int32, (count, ctx_dev), 0), slots)
        position = me_owner * ctx_dev + lax.broadcasted_iota(jnp.int32, (count, ctx_dev), 1)
        scores = jnp.full((count, ctx_dev), masked_fill, F32)
        limit = jnp.zeros((count, ctx_dev), jnp.int32)
        loads[5].wait()
        for s in range(seq_dev):
            raw = lax.dot_general(
                rotated,
                cache_v[s, :, :HEAD_DIM],
                (((1,), (1,)), ((), ())),
                preferred_element_type=F32,
            )
            limit = jnp.where(line == s, lengths_ref[s], limit)
            scores = jnp.where(line == s, raw * scale, scores)
        live = position < limit
        scores = jnp.where(live, scores, masked_fill)
        top = jnp.maximum(jnp.max(scores, 1, keepdims=True), own)
        weights = jnp.where(live, jnp.exp(scores - top), 0.0)
        own_weight = jnp.where(me_owner == 0, jnp.exp(own - top), 0.0)
        denom = jnp.sum(weights, 1, keepdims=True) + own_weight
        value = newkv[:, HEAD_DIM:]
        numer = own_weight * jnp.concatenate([value] * pairs, 0)
        for s in range(seq_dev):
            numer = numer + jnp.dot(
                jnp.where(line == s, weights, 0.0).astype(BF16),
                cache_v[s, :, HEAD_DIM:],
                preferred_element_type=F32,
            )
        for d in range(spots):
            side = jnp.zeros((rp, 128), F32)
            for j in range(pairs_dev):
                low = (d * pairs_dev + j) * rp
                for c in range(HEAD_DIM // 128):
                    part_v[d, j * (HEAD_DIM // 128) + c] = numer[
                        low : low + rp, c * 128 : (c + 1) * 128
                    ].astype(BF16)
                inner = lane % 32
                side = jnp.where((inner >= j * wide) & (inner < 16), top[low : low + rp], side)
                side = jnp.where(inner >= 16 + j * wide, denom[low : low + rp], side)
            pieces = []
            for c in range(2):
                scaled = side * 65537.0
                pieces.append(scaled - (scaled - side))
                side = side - pieces[-1]
            side = jnp.where(lane < 32, pieces[0], jnp.where(lane < 64, pieces[1], side))
            part_v[d, pairs_dev * (HEAD_DIM // 128)] = side.astype(BF16)
        mine = gy * owners + me_owner
        for offset in offsets:
            px, py, pz = shifted(*offset)
            send(
                part_v.at[py * ngz + pz],
                prs_v.at[mine],
                send_sem.at[4],
                recv_sem.at[4],
                at(px, py, pz),
            )
        prs_v[mine] = part_v[spot]

    def combine_parts():
        arrived(prs_v.at[pl.ds(0, ngy * owners - 1)], recv_sem.at[4])
        base = pairs_dev * (HEAD_DIM // 128)
        groups = []
        for y in range(ngy):
            sides = []
            for o in range(owners):
                k = y * owners + o
                side = prs_v[k, base].astype(F32)
                sides.append(side + rolled(side, -32, 1) + rolled(side, -64, 1))
            top = functools.reduce(jnp.maximum, sides)
            factors = [jnp.where(lane < 16, jnp.exp(side - top), 0.0) for side in sides]
            denom = functools.reduce(
                jnp.add, [rolled(f, 16, 1) * side for f, side in zip(factors, sides)]
            )
            share = rolled(1.0 / denom, -16, 1)
            factors = [f * share for f in factors]
            tiles = [None] * base
            for j in range(pairs_dev):
                for o in range(owners):
                    f = factors[o][:, j * wide : j * wide + 1]
                    for c in range(HEAD_DIM // 128):
                        t = j * (HEAD_DIM // 128) + c
                        piece = f * prs_v[y * owners + o, t].astype(F32)
                        tiles[t] = piece if tiles[t] is None else tiles[t] + piece
            groups.append(tiles)
        row = lax.broadcasted_iota(jnp.int32, (rp, 128), 0)
        for h in range(heads_dev):
            for c in range(HEAD_DIM // 128):
                total = jnp.zeros((rp, 128), F32)
                for y in range(ngy):
                    tile = groups[y][(h // 2) * (HEAD_DIM // 128) + c]
                    moved = rolled(tile, y * seq_dev - (h % 2) * slots, 0)
                    inside = (row >= y * seq_dev) & (row < (y + 1) * seq_dev)
                    total = jnp.where(inside, moved, total)
                low = h * HEAD_DIM + c * 128
                heads_v[:, low : low + 128] = total.astype(BF16)

    def hidden():
        arrived(grs_v.at[pl.ds(0, ngx - 1)], recv_sem.at[1])
        g = own_v[0]
        u = own_v[1]
        mean_drift = jnp.zeros((rp, 1), F32)
        for k in range(ngx):
            mean_drift = jnp.where(gx == k, drift[k], mean_drift)
        g = g + mean_drift * g[rows : rows + 1, :]
        u = u + mean_drift * u[rows : rows + 1, :]
        for j in range(ngx - 1):
            peer = other(j)
            shift = jnp.where(gx <= j, drift[j + 1], drift[j])
            g_part = grs_v[peer, 0].astype(F32)
            u_part = grs_v[peer, 1].astype(F32)
            g = g + g_part + shift * g_part[rows : rows + 1, :]
            u = u + u_part + shift * u_part[rows : rows + 1, :]
        g = g * inverse
        u = u * inverse
        hid_v[gx] = (g / (1.0 + jnp.exp(-g)) * u).astype(BF16)
        for j in range(ngx - 1):
            send(hid_v.at[gx], hid_v.at[gx], send_sem.at[5], h_recv.at[gx], at(other(j), gy, gz))

    def down_product(step):
        source = source_at(step)
        if step:
            arrived(hid_v.at[source], h_recv.at[source])
        down_copy(step).wait()
        product = jnp.dot(hid_v[source], down_v[step], preferred_element_type=F32)
        if step:
            acc_v[...] += product
        else:
            acc_v[...] = product

    peers = [o for o in itertools.product(range(ngy), range(ngz)) if any(o)]

    def scoped(name, f, *args):
        with jax.named_scope(name):
            return f(*args)

    scoped("gu0", gate_up, 0)
    drift, inverse = scoped("moments", moments)
    scoped("gatherq", gather_query)
    for step in range(1, ngx - 1):
        scoped("gu%d" % step, gate_up, step)
    scoped("attend", attend)
    scoped("gulast", gate_up, ngx - 1)
    scoped("hidden", hidden)
    for step in range(ngx - 1):
        scoped("down%d" % step, down_product, step)
    scoped("combine", combine_parts)

    def out_product():
        loads[6].wait()
        acc_v[...] += jnp.dot(heads_v[...], out_v[...], preferred_element_type=F32)

    scoped("outp", out_product)

    def last_down():
        source = source_at(ngx - 1)
        arrived(hid_v.at[source], h_recv.at[source])
        down_copy(ngx - 1).wait()
        for part in range(2):
            columns = slice(part * half, (part + 1) * half)
            acc_v[:, columns] += jnp.dot(
                hid_v[source], down_v[ngx - 1, :, columns], preferred_element_type=F32
            )
            fin_v[part, spot] = acc_v[:, columns].astype(BF16)
            for oy, oz in peers:
                px, py, pz = shifted(0, oy, oz)
                send(
                    fin_v.at[part, spot],
                    fin_v.at[part, spot],
                    send_sem.at[6],
                    f_recv.at[part],
                    at(px, py, pz),
                )

    scoped("lastdown", last_down)

    def final():
        for part in range(2):
            columns = slice(part * half, (part + 1) * half)
            total = x_v[:, columns] + acc_v[:, columns]
            arrived(fin_v.at[part, pl.ds(0, spots - 1)], f_recv.at[part])
            for oy, oz in peers:
                px, py, pz = shifted(0, oy, oz)
                total = total + fin_v[part, py * ngz + pz].astype(F32)
            mixed_ref[:, columns] = total[:rows].astype(BF16)

    scoped("final", final)

    def drain():
        left(r1_v.at[pl.ds(0, ngx - 1)], send_sem.at[0])
        left(gsend_v, send_sem.at[1])
        left(qall_v.at[pl.ds(0, HEADS - own_heads)], send_sem.at[2])
        left(kvq_v.at[pl.ds(0, spots - 1)], send_sem.at[3])
        left(prs_v.at[pl.ds(0, ngy * owners - 1)], send_sem.at[4])
        left(hid_v.at[pl.ds(0, ngx - 1)], send_sem.at[5])
        left(fin_v.at[:, pl.ds(0, spots - 1)], send_sem.at[6])

    scoped("drain", drain)


def fused(sizes, *args):
    (tokens, gain, qw, kvw, outw, gatew, upw, downw, cache, lengths) = args
    ngx, ngy, ngz = sizes
    rows, dx = tokens.shape
    rp = (rows // 8 + 1) * 8
    qd = qw.shape[1]
    fb = gatew.shape[1] // ngx
    heads_dev = qd // HEAD_DIM
    own_heads = heads_dev // ngx
    qo = own_heads * HEAD_DIM
    owners = ngx * ngz
    spots = ngy * ngz
    kw = kvw.shape[1] // spots
    middle = HEAD_DIM // 2
    tiles = heads_dev // 2 * (HEAD_DIM // 128) + 1
    spread = np.power(
        np.float32(rotary_base), -np.arange(middle, dtype=np.float32) / np.float32(middle)
    ).reshape(1, middle)
    dma = pltpu.SemaphoreType.DMA
    vm = pltpu.VMEM
    scratch = [
        pltpu.SMEM(lengths.shape, jnp.int32),
        vm(tokens.shape, BF16),
        vm((1, dx), F32),
        vm((1, middle), F32),
        vm(qw.shape, BF16),
        vm((dx, kw), BF16),
        vm(cache.shape, BF16),
        vm((ngx, 2, dx, fb), BF16),
        vm(outw.shape, BF16),
        vm((ngx, fb, dx), BF16),
        dma((8,)),
        dma((ngx,)),
        dma((ngx,)),
        vm((rp, dx), F32),
        vm((rp, dx), BF16),
        vm((ngx, rp, qo + kw + 128), F32),
        vm((ngx, rp, qo + kw + 128), F32),
        vm((ngy, rp, kw), F32),
        vm((spots, rp, kw), F32),
        vm((ngy, own_heads, rp, HEAD_DIM), BF16),
        vm((HEADS, rp, HEAD_DIM), BF16),
        vm((HEADS // 2, rp, HEAD_DIM), F32),
        vm((spots, tiles, rp, 128), BF16),
        vm((ngy * owners, tiles, rp, 128), BF16),
        vm((ngx - 1, 2, rp, fb), BF16),
        vm((ngx, 2, rp, fb), BF16),
        vm((2, rp, fb), F32),
        vm((ngx, rp, fb), BF16),
        vm((rp, dx), F32),
        vm((rp, qd), BF16),
        vm((2, spots, rp, dx // 2), BF16),
        dma((7,)),
        dma((5,)),
        dma((ngx,)),
        dma((2,)),
    ]
    anywhere = pl.BlockSpec(memory_space=pl.ANY)
    return pl.pallas_call(
        functools.partial(kernel, (ngx, ngy, ngz, rows, rp)),
        out_shape=(
            pltpu.VMEM(tokens.shape, BF16),
            pltpu.VMEM((cache.shape[0], 2 * HEAD_DIM), BF16),
        ),
        in_specs=[anywhere] * 11,
        out_specs=(pl.BlockSpec(memory_space=pltpu.VMEM),) * 2,
        scratch_shapes=scratch,
        compiler_params=pltpu.CompilerParams(
            collective_id=0, has_side_effects=True, vmem_limit_bytes=61 * 2**20
        ),
    )(lengths, tokens, gain.reshape(1, dx), spread, qw, kvw, cache, gatew, upw, outw, downw)


def fits(sizes, rows, seq_dev, d_dev, q_dev, ff_dev, weight_bytes):
    ngx, ngy, ngz = sizes
    heads_dev = q_dev // HEAD_DIM
    return (
        ngx >= 3
        and rows < 8
        and rows == ngy * seq_dev
        and seq_dev <= 4
        and heads_dev in (2, 4, 8)
        and heads_dev * ngy * ngz == HEADS
        and d_dev % 1024 == 0
        and heads_dev % ngx == 0
        and 2 * HEAD_DIM % (ngy * ngz * 128) == 0
        and ff_dev % (ngx * 128) == 0
        and weight_bytes <= 60 * 2**20
    )


def choose(sizes, *args):
    held = sum(a.size * a.dtype.itemsize for a in args[2:9])
    rows, d_dev = args[0].shape
    seq_dev = args[8].shape[0]
    if fits(sizes, rows, seq_dev, d_dev, args[2].shape[1], args[5].shape[1], held):
        return fused(sizes, *args)
    return body(*args)


def solution(mesh):
    sizes = tuple(mesh.shape[a] for a in ("gx", "gy", "gz"))
    chosen = functools.partial(choose, sizes)
    in_specs = (
        P("group", "gx"),
        P("gx"),
        P("gx", ("gy", "gz")),
        P("gx", None),
        P(("gy", "gz"), "gx"),
        P("gx", ("gy", "gz")),
        P("gx", ("gy", "gz")),
        P(("gy", "gz"), "gx"),
        P(("group", "gy"), ("gx", "gz"), None),
        P(("group", "gy")),
    )
    out_specs = (P("group", "gx"), P(("group", "gy"), None))
    return jax.shard_map(chosen, mesh=mesh, in_specs=in_specs, out_specs=out_specs, check_vma=False)
```

```python
import functools
import itertools

import jax
import jax.numpy as jnp
import numpy as np
from jax import lax
from jax.experimental import pallas as pl
from jax.experimental.pallas import tpu as pltpu
from jax.sharding import PartitionSpec as P

D = 8192
HEADS = 16
HEAD_DIM = 256


epsilon = 1e-05
masked_fill = -1e30
rotary_base = 10000.0


def joined(part, axis, combine):
    gathered = jax.tree.map(lambda a: lax.all_gather(a, axis), part)

    def take(source):
        return jax.tree.map(lambda a: lax.dynamic_index_in_dim(a, source, 0, False), gathered)

    return lax.fori_loop(
        1, lax.axis_size(axis), lambda source, state: combine(state, take(source)), take(0)
    )


def rotate(values, angle):
    middle = values.shape[-1] // 2
    first = values[..., :middle]
    second = values[..., middle:]
    cosine = jnp.cos(angle)
    sine_part = jnp.sin(angle)
    return jnp.concatenate(
        [first * cosine - second * sine_part, first * sine_part + second * cosine], -1
    )


def angles(lengths, head_dim):
    middle = head_dim // 2
    spread = rotary_base ** (-jnp.arange(middle, dtype=jnp.float32) / middle)
    return lengths.astype(jnp.float32)[:, None] * spread[None, :]


def combine(earlier, later):
    top = jnp.maximum(earlier[0], later[0])
    first_scale = jnp.exp(earlier[0] - top)
    second_scale = jnp.exp(later[0] - top)
    numer = earlier[1] * first_scale[..., None] + later[1] * second_scale[..., None]
    denom = earlier[2] * first_scale + later[2] * second_scale
    return (top, numer, denom)


def body(
    tokens,
    norm_gain,
    q_weight,
    kv_weight,
    out_weight,
    gate_weight,
    up_weight,
    down_weight,
    kv_cache,
    lengths,
):
    inputs = tokens.astype(jnp.float32)
    totals = lax.psum((jnp.sum(inputs, 1), jnp.sum(inputs * inputs, 1)), "gx")
    center = totals[0] / D
    spread_sq = totals[1] / D - center * center
    normed = (
        (inputs - center[:, None]) * lax.rsqrt(spread_sq + epsilon)[:, None] * norm_gain[None, :]
    ).astype(jnp.bfloat16)
    query_part = jnp.dot(normed, q_weight, preferred_element_type=jnp.float32)
    keyval_part = jnp.dot(normed, kv_weight, preferred_element_type=jnp.float32)
    gate_part = jnp.dot(normed, gate_weight, preferred_element_type=jnp.float32)
    up_part = jnp.dot(normed, up_weight, preferred_element_type=jnp.float32)
    query, keyval, gate, upward = lax.psum((query_part, keyval_part, gate_part, up_part), "gx")
    hidden = (jax.nn.silu(gate) * upward).astype(jnp.bfloat16)
    seq_dev = lengths.shape[0]
    row_groups = lax.axis_size("gy")
    block = q_weight.shape[1]
    first_row = lax.axis_index("gy") * seq_dev
    angle = angles(lengths, HEAD_DIM)
    own_keyval = lax.dynamic_slice_in_dim(keyval, first_row, seq_dev, 0)
    new_kv = jnp.concatenate(
        [rotate(own_keyval[:, :HEAD_DIM], angle), own_keyval[:, HEAD_DIM:]], 1
    ).astype(jnp.bfloat16)
    query_bf = query.astype(jnp.bfloat16)
    every_head = lax.all_gather(query_bf, ("gy", "gz"), axis=1, tiled=True)
    own_query = lax.dynamic_slice_in_dim(every_head, first_row, seq_dev, 0)
    rotated = rotate(
        own_query.astype(jnp.float32).reshape(seq_dev, HEADS, HEAD_DIM), angle[:, None, :]
    ).astype(jnp.bfloat16)
    ctx_dev = kv_cache.shape[1]
    offset = lax.axis_index(("gx", "gz")) * ctx_dev
    positions = offset + jnp.arange(ctx_dev, dtype=jnp.int32)
    live = positions[None, :] < lengths[:, None]
    scale = HEAD_DIM ** (-0.5)
    scores = (
        jnp.einsum(
            "shd,scd->shc", rotated, kv_cache[:, :, :HEAD_DIM], preferred_element_type=jnp.float32
        )
        * scale
    )
    key_new = new_kv[:, :HEAD_DIM]
    value_new = new_kv[:, HEAD_DIM:]
    own_score = (
        jnp.einsum("shd,sd->sh", rotated, key_new, preferred_element_type=jnp.float32) * scale
    )
    hidden_scores = jnp.where(live[:, None, :], scores, masked_fill)
    local_top = jnp.maximum(jnp.max(hidden_scores, 2), own_score)
    weights = jnp.where(live[:, None, :], jnp.exp(hidden_scores - local_top[..., None]), 0.0)
    numer = jnp.einsum(
        "shc,scd->shd",
        weights.astype(jnp.bfloat16),
        kv_cache[:, :, HEAD_DIM:],
        preferred_element_type=jnp.float32,
    )
    denom = jnp.sum(weights, 2)
    top, numer, denom = joined((local_top, numer, denom), ("gx", "gz"), combine)
    own_weight = jnp.exp(own_score - top)
    numer = numer + own_weight[..., None] * value_new.astype(jnp.float32)[:, None, :]
    denom = denom + own_weight
    attended = (numer / denom[..., None]).astype(jnp.bfloat16)
    grouped = attended.reshape(seq_dev, row_groups, HEADS * HEAD_DIM // row_groups)
    picked = lax.dynamic_slice_in_dim(grouped, lax.axis_index("gz") * block, block, 2)
    head_block = lax.all_to_all(picked, "gy", split_axis=1, concat_axis=0, tiled=True).reshape(
        seq_dev * row_groups, block
    )
    partial_value = jnp.dot(head_block, out_weight, preferred_element_type=jnp.float32) + jnp.dot(
        hidden, down_weight, preferred_element_type=jnp.float32
    )
    total = lax.psum(partial_value, ("gy", "gz"))
    mixed = (inputs + total).astype(jnp.bfloat16)
    return (mixed, new_kv)


MESH = pl.DeviceIdType.MESH
F32 = jnp.float32
BF16 = jnp.bfloat16


def kernel(
    dims,
    lengths_h,
    tokens_h,
    gain_h,
    spread_h,
    q_h,
    kv_h,
    cache_h,
    gate_h,
    up_h,
    out_h,
    down_h,
    mixed_ref,
    newkv_ref,
    lengths_ref,
    tokens_v,
    gain_v,
    spread_v,
    q_v,
    kv_v,
    cache_v,
    gu_v,
    out_v,
    down_v,
    load_sem,
    gu_sem,
    down_sem,
    x_v,
    normed_v,
    s1_v,
    r1_v,
    kvs_v,
    kvq_v,
    qsend_v,
    qall_v,
    rot_v,
    part_v,
    prs_v,
    gsend_v,
    grs_v,
    own_v,
    hid_v,
    acc_v,
    heads_v,
    fin_v,
    send_sem,
    recv_sem,
    h_recv,
    f_recv,
):
    ngx, ngy, ngz, rows, rp = dims
    gx, gy, gz = lax.axis_index("gx"), lax.axis_index("gy"), lax.axis_index("gz")
    dx = x_v.shape[1]
    qd = q_v.shape[1]
    heads_dev = qd // HEAD_DIM
    own_heads = heads_dev // ngx
    qo = own_heads * HEAD_DIM
    kw = kv_v.shape[1]
    seq_dev = cache_v.shape[0]
    ctx_dev = cache_v.shape[1]
    fb = gu_v.shape[3]
    owners = ngx * ngz
    spots = ngy * ngz
    pairs = HEADS // 2
    pairs_dev = heads_dev // 2
    slots = rp // 2
    wide = 16 // pairs_dev
    scale = HEAD_DIM ** (-0.5)
    middle = HEAD_DIM // 2
    half = dx // 2
    me_owner = gx * ngz + gz
    spot = gy * ngz + gz

    def rolled(values, shift, axis):
        shift = shift % values.shape[axis]
        return pltpu.roll(values, shift, axis) if shift else values

    lane = lax.broadcasted_iota(jnp.int32, (rp, 128), 1)

    def split_three(values):
        pieces = []
        for c in range(2):
            scaled = values * 65537.0
            pieces.append(scaled - (scaled - values))
            values = values - pieces[-1]
        return jnp.where(lane < 32, pieces[0], jnp.where(lane < 64, pieces[1], values))

    def join_three(pieces):
        pieces = pieces.astype(F32)
        return pieces + rolled(pieces, -32, 1) + rolled(pieces, -64, 1)

    def other(j):
        return jnp.where(gx <= j, j + 1, j)

    def block_at(step):
        return gx if step == ngx - 1 else other(step)

    def source_at(step):
        return gx if step == 0 else other(step - 1)

    def columns_of(block, width):
        return pl.ds(pl.multiple_of(block * width, width), width)

    loads = [
        pltpu.make_async_copy(a, b, load_sem.at[i])
        for i, (a, b) in enumerate(
            (
                (tokens_h, tokens_v),
                (gain_h, gain_v),
                (spread_h, spread_v),
                (kv_h.at[:, columns_of(spot, kw)], kv_v),
                (q_h, q_v),
                (cache_h, cache_v),
                (out_h, out_v),
                (lengths_h, lengths_ref),
            )
        )
    ]

    def gu_start(step):
        columns = columns_of(block_at(step), fb)
        pltpu.make_async_copy(gate_h.at[:, columns], gu_v.at[step, 0], gu_sem.at[0, step]).start()
        pltpu.make_async_copy(up_h.at[:, columns], gu_v.at[step, 1], gu_sem.at[1, step]).start()

    def down_copy(step):
        picked = columns_of(source_at(step), fb)
        return pltpu.make_async_copy(down_h.at[picked], down_v.at[step], down_sem.at[step])

    offsets = [o for o in itertools.product(range(ngx), range(ngy), range(ngz)) if any(o)]

    def shifted(ox, oy, oz):
        return lax.rem(gx + ox, ngx), lax.rem(gy + oy, ngy), lax.rem(gz + oz, ngz)

    def at(px, py, pz):
        return {"gx": px, "gy": py, "gz": pz}

    barrier = pltpu.get_barrier_semaphore()
    for offset in offsets:
        pl.semaphore_signal(barrier, inc=1, device_id=at(*shifted(*offset)), device_id_type=MESH)

    for i in (0, 1, 2, 7, 3, 4):
        loads[i].start()

    sc0 = jax.named_scope('begin')
    sc0.__enter__()
    loads[0].wait()
    gu_start(0)
    x_v[...] = jnp.zeros_like(x_v)
    x_v[0:rows, :] = tokens_v[...].astype(F32)
    x = x_v[...]
    sums = jnp.sum(x, 1, keepdims=True)
    stat = jnp.where(lane % 32 < 16, sums, jnp.sum(x * x, 1, keepdims=True))
    stat = split_three(stat).astype(BF16)
    loads[1].wait()
    gu_start(1)
    spare = lax.broadcasted_iota(jnp.int32, (rp, dx), 0) == rows
    centred = jnp.where(spare, 1.0, x - sums / dx)
    normed_v[...] = (centred * gain_v[...]).astype(BF16)

    loads[2].wait()
    loads[7].wait()
    loads[5].start()
    line = lax.rem(lax.broadcasted_iota(jnp.int32, (rp, middle), 0), slots)
    length = jnp.zeros((rp, middle), jnp.int32)
    for s in range(seq_dev):
        length = jnp.where(line == s, lengths_ref[s], length)
    angle = length.astype(F32) * spread_v[...]
    cosine = jnp.cos(angle)
    sine = jnp.sin(angle)

    sc0.__exit__(None, None, None)
    sc0 = jax.named_scope('qdot')
    sc0.__enter__()
    loads[3].wait()
    gu_start(2)
    kv_part = jnp.dot(normed_v[...], kv_v[...], preferred_element_type=F32)
    loads[4].wait()
    for step in range(3, ngx):
        gu_start(step)
    q_part = jnp.dot(normed_v[...], q_v[...], preferred_element_type=F32)
    for j in range(ngx):
        s1_v[j, :, :qo] = q_part[:, j * qo : (j + 1) * qo].astype(BF16)
        s1_v[j, :, qo : qo + kw] = kv_part.astype(BF16)
        s1_v[j, :, qo + kw :] = stat

    sc0.__exit__(None, None, None)
    with jax.named_scope('barrier'):
        pl.semaphore_wait(barrier, len(offsets))

    def send(source, target, sends, receives, device):
        pltpu.make_async_remote_copy(
            src_ref=source,
            dst_ref=target,
            send_sem=sends,
            recv_sem=receives,
            device_id=device,
            device_id_type=MESH,
        ).start()

    def arrival(slot, semaphore):
        return pltpu.make_async_remote_copy(
            src_ref=slot,
            dst_ref=slot,
            send_sem=semaphore,
            recv_sem=semaphore,
            device_id=at(gx, gy, gz),
            device_id_type=MESH,
        )

    def arrived(slot, semaphore):
        arrival(slot, semaphore).wait_recv()

    def left(slot, semaphore):
        arrival(slot, semaphore).wait_send()

    for k in range(1, ngx):
        peer = lax.rem(gx + k, ngx)
        send(s1_v.at[peer], r1_v.at[gx], send_sem.at[0], recv_sem.at[0], at(peer, gy, gz))
    r1_v[gx] = s1_v[gx]

    def later_loads(k):
        if k == 0:
            down_copy(0).start()
        elif k == 1:
            loads[6].start()
        elif k - 1 < ngx:
            down_copy(k - 1).start()

    def gate_up(step):
        for which in range(2):
            slot = gu_v.at[step, which]
            pltpu.make_async_copy(slot, slot, gu_sem.at[which, step]).wait()
            later_loads(2 * step + which)
            part = jnp.dot(normed_v[...], gu_v[step, which], preferred_element_type=F32)
            if step < ngx - 1:
                gsend_v[step, which] = part.astype(BF16)
            else:
                own_v[which] = part
        if step < ngx - 1:
            send(
                gsend_v.at[step],
                grs_v.at[gx],
                send_sem.at[1],
                recv_sem.at[1],
                at(block_at(step), gy, gz),
            )

    def moments():
        arrived(r1_v.at[pl.ds(0, ngx - 1)], recv_sem.at[0])
        stats = [join_three(r1_v[k, :, qo + kw :]) for k in range(ngx)]
        totals = functools.reduce(jnp.add, stats)
        center = totals[:, 0:1] / D
        spread_sq = totals[:, 16:17] / D - center * center
        drift = [part[:, 0:1] / dx - center for part in stats]
        return drift, lax.rsqrt(spread_sq + epsilon)

    row = lax.broadcasted_iota(jnp.int32, (rp, 128), 0)
    above = row < slots

    def packed(values, y):
        upper = rolled(values, -y * seq_dev, 0)
        lower = rolled(values, slots - y * seq_dev, 0)
        keep = lax.broadcasted_iota(jnp.int32, values.shape, 0) < slots
        return jnp.where(keep, upper, lower)

    def gather_query():
        total = None
        for k in range(ngx):
            values = r1_v[k, :, : qo + kw].astype(F32)
            part = values + drift[k] * values[rows : rows + 1, :]
            total = part if total is None else total + part
        total = total * inverse
        mine = spot * heads_dev + gx * own_heads
        for y in range(ngy):
            for h in range(own_heads):
                low = h * HEAD_DIM
                upper = rolled(total[:, low : low + middle], -y * seq_dev, 0)
                lower = rolled(total[:, low + middle : low + HEAD_DIM], slots - y * seq_dev, 0)
                qsend_v[y, h] = jnp.where(above, upper, lower).astype(BF16)
            kvs_v[y] = packed(total[:, qo:], y)
        for offset in offsets:
            px, py, pz = shifted(*offset)
            send(
                qsend_v.at[py],
                qall_v.at[pl.ds(mine, own_heads)],
                send_sem.at[2],
                recv_sem.at[2],
                at(px, py, pz),
            )
            if not offset[0]:
                send(kvs_v.at[py], kvq_v.at[spot], send_sem.at[3], recv_sem.at[3], at(px, py, pz))
        for h in range(own_heads):
            qall_v[mine + h] = qsend_v[gy, h]
        kvq_v[spot] = kvs_v[gy]

    fold = pairs_dev * (HEAD_DIM // 128) == slots and seq_dev == slots - 1
    base = pairs_dev * (HEAD_DIM // 128) - fold

    def folded(tiles, t):
        if not fold:
            return tiles[t]
        return jnp.where(row % slots == slots - 1, rolled(tiles[-1], slots - 1 - t, 0), tiles[t])

    def unfolded(tiles):
        if not fold:
            return tiles
        last = rolled(tiles[0], 1 - slots, 0)
        for t in range(1, base):
            last = jnp.where(row % slots == t, rolled(tiles[t], t + 1 - slots, 0), last)
        return tiles + [last]

    def attend():
        arrived(kvq_v.at[pl.ds(0, spots - 1)], recv_sem.at[3])
        keyval = jnp.concatenate([kvq_v[k] for k in range(spots)], 1)
        a = keyval[:, :middle]
        b = keyval[:, middle:HEAD_DIM]
        newkv = jnp.concatenate(
            [a * cosine - b * sine, a * sine + b * cosine, keyval[:, HEAD_DIM:]], 1
        ).astype(BF16)
        newkv_ref[...] = newkv[:seq_dev]
        newkv = newkv.astype(F32)
        arrived(qall_v.at[pl.ds(0, HEADS - own_heads)], recv_sem.at[2])
        owns = []
        for p in range(pairs):
            even = qall_v[2 * p].astype(F32)
            odd = qall_v[2 * p + 1].astype(F32)
            a = jnp.where(above, even, rolled(odd, slots, 0))
            b = jnp.where(above, rolled(even, slots, 0), odd)
            first = (a * cosine - b * sine).astype(BF16).astype(F32)
            second = (a * sine + b * cosine).astype(BF16).astype(F32)
            rot_v[p, :, :middle] = first
            rot_v[p, :, middle:] = second
            product = first * newkv[:, :middle] + second * newkv[:, middle:HEAD_DIM]
            owns.append(jnp.sum(product, 1, keepdims=True) * scale)
        count = pairs * rp
        rotated = rot_v[...].reshape(count, HEAD_DIM).astype(BF16)
        own = jnp.where(me_owner == 0, jnp.concatenate(owns, 0), masked_fill)
        line = lax.rem(lax.broadcasted_iota(jnp.int32, (count, ctx_dev), 0), slots)
        position = me_owner * ctx_dev + lax.broadcasted_iota(jnp.int32, (count, ctx_dev), 1)
        scores = jnp.full((count, ctx_dev), masked_fill, F32)
        limit = jnp.zeros((count, ctx_dev), jnp.int32)
        loads[5].wait()
        for s in range(seq_dev):
            raw = lax.dot_general(
                rotated,
                cache_v[s, :, :HEAD_DIM],
                (((1,), (1,)), ((), ())),
                preferred_element_type=F32,
            )
            limit = jnp.where(line == s, lengths_ref[s], limit)
            scores = jnp.where(line == s, raw * scale, scores)
        live = position < limit
        scores = jnp.where(live, scores, masked_fill)
        top = jnp.maximum(jnp.max(scores, 1, keepdims=True), own)
        weights = jnp.where(live, jnp.exp(scores - top), 0.0)
        own_weight = jnp.where(me_owner == 0, jnp.exp(own - top), 0.0)
        denom = jnp.sum(weights, 1, keepdims=True) + own_weight
        value = newkv[:, HEAD_DIM:]
        numer = own_weight * jnp.concatenate([value] * pairs, 0)
        for s in range(seq_dev):
            numer = numer + jnp.dot(
                jnp.where(line == s, weights, 0.0).astype(BF16),
                cache_v[s, :, HEAD_DIM:],
                preferred_element_type=F32,
            )
        for d in range(spots):
            side = jnp.zeros((rp, 128), F32)
            tiles = []
            for j in range(pairs_dev):
                low = (d * pairs_dev + j) * rp
                for c in range(HEAD_DIM // 128):
                    tiles.append(numer[low : low + rp, c * 128 : (c + 1) * 128])
                inner = lane % 32
                side = jnp.where((inner >= j * wide) & (inner < 16), top[low : low + rp], side)
                side = jnp.where(inner >= 16 + j * wide, denom[low : low + rp], side)
            for t in range(base):
                part_v[d, t] = folded(tiles, t).astype(BF16)
            part_v[d, base] = split_three(side).astype(BF16)
        mine = gy * owners + me_owner
        for offset in offsets:
            px, py, pz = shifted(*offset)
            send(
                part_v.at[py * ngz + pz],
                prs_v.at[mine],
                send_sem.at[4],
                recv_sem.at[4],
                at(px, py, pz),
            )
        prs_v[mine] = part_v[spot]

    def combine_parts():
        arrived(prs_v.at[pl.ds(0, ngy * owners - 1)], recv_sem.at[4])
        groups = []
        for y in range(ngy):
            sides = []
            for o in range(owners):
                k = y * owners + o
                sides.append(join_three(prs_v[k, base]))
            top = functools.reduce(jnp.maximum, sides)
            factors = [jnp.where(lane < 16, jnp.exp(side - top), 0.0) for side in sides]
            denom = functools.reduce(
                jnp.add, [rolled(f, 16, 1) * side for f, side in zip(factors, sides)]
            )
            share = rolled(1.0 / denom, -16, 1)
            factors = [f * share for f in factors]
            tiles = [None] * (base + fold)
            for o in range(owners):
                pieces = unfolded([prs_v[y * owners + o, t].astype(F32) for t in range(base)])
                for j in range(pairs_dev):
                    f = factors[o][:, j * wide : j * wide + 1]
                    for c in range(HEAD_DIM // 128):
                        t = j * (HEAD_DIM // 128) + c
                        piece = f * pieces[t]
                        tiles[t] = piece if tiles[t] is None else tiles[t] + piece
            groups.append(tiles)
        for h in range(heads_dev):
            for c in range(HEAD_DIM // 128):
                total = jnp.zeros((rp, 128), F32)
                for y in range(ngy):
                    tile = groups[y][(h // 2) * (HEAD_DIM // 128) + c]
                    moved = rolled(tile, y * seq_dev - (h % 2) * slots, 0)
                    inside = (row >= y * seq_dev) & (row < (y + 1) * seq_dev)
                    total = jnp.where(inside, moved, total)
                low = h * HEAD_DIM + c * 128
                heads_v[:, low : low + 128] = total.astype(BF16)

    def hidden():
        arrived(grs_v.at[pl.ds(0, ngx - 1)], recv_sem.at[1])
        g = own_v[0]
        u = own_v[1]
        mean_drift = jnp.zeros((rp, 1), F32)
        for k in range(ngx):
            mean_drift = jnp.where(gx == k, drift[k], mean_drift)
        g = g + mean_drift * g[rows : rows + 1, :]
        u = u + mean_drift * u[rows : rows + 1, :]
        for j in range(ngx - 1):
            peer = other(j)
            shift = jnp.where(gx <= j, drift[j + 1], drift[j])
            g_part = grs_v[peer, 0].astype(F32)
            u_part = grs_v[peer, 1].astype(F32)
            g = g + g_part + shift * g_part[rows : rows + 1, :]
            u = u + u_part + shift * u_part[rows : rows + 1, :]
        g = g * inverse
        u = u * inverse
        hid_v[gx] = (g / (1.0 + jnp.exp(-g)) * u).astype(BF16)
        for j in range(ngx - 1):
            send(hid_v.at[gx], hid_v.at[gx], send_sem.at[5], h_recv.at[gx], at(other(j), gy, gz))

    def down_product(step):
        source = source_at(step)
        if step:
            arrived(hid_v.at[source], h_recv.at[source])
        down_copy(step).wait()
        product = jnp.dot(hid_v[source], down_v[step], preferred_element_type=F32)
        if step:
            acc_v[...] += product
        else:
            acc_v[...] = product

    peers = [o for o in itertools.product(range(ngy), range(ngz)) if any(o)]

    def scoped(name, f, *args):
        with jax.named_scope(name):
            return f(*args)

    scoped("gu0", gate_up, 0)
    drift, inverse = scoped("moments", moments)
    scoped("gatherq", gather_query)
    for step in range(1, ngx - 1):
        scoped("gu%d" % step, gate_up, step)
    scoped("attend", attend)
    scoped("gulast", gate_up, ngx - 1)
    scoped("hidden", hidden)
    scoped("down0", down_product, 0)
    scoped("combine", combine_parts)

    def out_product():
        loads[6].wait()
        acc_v[...] += jnp.dot(heads_v[...], out_v[...], preferred_element_type=F32)

    scoped("outp", out_product)
    for step in range(1, ngx - 1):
        scoped("down%d" % step, down_product, step)

    def last_down():
        source = source_at(ngx - 1)
        arrived(hid_v.at[source], h_recv.at[source])
        down_copy(ngx - 1).wait()
        for part in range(2):
            columns = slice(part * half, (part + 1) * half)
            acc_v[:, columns] += jnp.dot(
                hid_v[source], down_v[ngx - 1, :, columns], preferred_element_type=F32
            )
            fin_v[part, spot] = acc_v[:, columns].astype(BF16)
            for oy, oz in peers:
                px, py, pz = shifted(0, oy, oz)
                send(
                    fin_v.at[part, spot],
                    fin_v.at[part, spot],
                    send_sem.at[6],
                    f_recv.at[part],
                    at(px, py, pz),
                )

    scoped("lastdown", last_down)

    def final():
        for part in range(2):
            columns = slice(part * half, (part + 1) * half)
            total = x_v[:, columns] + acc_v[:, columns]
            arrived(fin_v.at[part, pl.ds(0, spots - 1)], f_recv.at[part])
            for oy, oz in peers:
                px, py, pz = shifted(0, oy, oz)
                total = total + fin_v[part, py * ngz + pz].astype(F32)
            mixed_ref[:, columns] = total[:rows].astype(BF16)

    scoped("final", final)

    def drain():
        left(r1_v.at[pl.ds(0, ngx - 1)], send_sem.at[0])
        left(gsend_v, send_sem.at[1])
        left(qall_v.at[pl.ds(0, HEADS - own_heads)], send_sem.at[2])
        left(kvq_v.at[pl.ds(0, spots - 1)], send_sem.at[3])
        left(prs_v.at[pl.ds(0, ngy * owners - 1)], send_sem.at[4])
        left(hid_v.at[pl.ds(0, ngx - 1)], send_sem.at[5])
        left(fin_v.at[:, pl.ds(0, spots - 1)], send_sem.at[6])

    scoped("drain", drain)


def fused(sizes, *args):
    (tokens, gain, qw, kvw, outw, gatew, upw, downw, cache, lengths) = args
    ngx, ngy, ngz = sizes
    rows, dx = tokens.shape
    rp = (rows // 8 + 1) * 8
    qd = qw.shape[1]
    fb = gatew.shape[1] // ngx
    heads_dev = qd // HEAD_DIM
    own_heads = heads_dev // ngx
    qo = own_heads * HEAD_DIM
    owners = ngx * ngz
    spots = ngy * ngz
    kw = kvw.shape[1] // spots
    middle = HEAD_DIM // 2
    slots = rp // 2
    tiles = heads_dev // 2 * (HEAD_DIM // 128)
    fold = tiles == slots and cache.shape[0] == slots - 1
    tiles = tiles - fold + 1
    spread = np.power(
        np.float32(rotary_base), -np.arange(middle, dtype=np.float32) / np.float32(middle)
    ).reshape(1, middle)
    dma = pltpu.SemaphoreType.DMA
    vm = pltpu.VMEM
    scratch = [
        pltpu.SMEM(lengths.shape, jnp.int32),
        vm(tokens.shape, BF16),
        vm((1, dx), F32),
        vm((1, middle), F32),
        vm(qw.shape, BF16),
        vm((dx, kw), BF16),
        vm(cache.shape, BF16),
        vm((ngx, 2, dx, fb), BF16),
        vm(outw.shape, BF16),
        vm((ngx, fb, dx), BF16),
        dma((8,)),
        dma((2, ngx)),
        dma((ngx,)),
        vm((rp, dx), F32),
        vm((rp, dx), BF16),
        vm((ngx, rp, qo + kw + 128), BF16),
        vm((ngx, rp, qo + kw + 128), BF16),
        vm((ngy, rp, kw), F32),
        vm((spots, rp, kw), F32),
        vm((ngy, own_heads, rp, middle), BF16),
        vm((HEADS, rp, middle), BF16),
        vm((HEADS // 2, rp, HEAD_DIM), F32),
        vm((spots, tiles, rp, 128), BF16),
        vm((ngy * owners, tiles, rp, 128), BF16),
        vm((ngx - 1, 2, rp, fb), BF16),
        vm((ngx, 2, rp, fb), BF16),
        vm((2, rp, fb), F32),
        vm((ngx, rp, fb), BF16),
        vm((rp, dx), F32),
        vm((rp, qd), BF16),
        vm((2, spots, rp, dx // 2), BF16),
        dma((7,)),
        dma((5,)),
        dma((ngx,)),
        dma((2,)),
    ]
    anywhere = pl.BlockSpec(memory_space=pl.ANY)
    return pl.pallas_call(
        functools.partial(kernel, (ngx, ngy, ngz, rows, rp)),
        out_shape=(
            pltpu.VMEM(tokens.shape, BF16),
            pltpu.VMEM((cache.shape[0], 2 * HEAD_DIM), BF16),
        ),
        in_specs=[anywhere] * 11,
        out_specs=(pl.BlockSpec(memory_space=pltpu.VMEM),) * 2,
        scratch_shapes=scratch,
        compiler_params=pltpu.CompilerParams(
            collective_id=0, has_side_effects=True, vmem_limit_bytes=61 * 2**20
        ),
    )(lengths, tokens, gain.reshape(1, dx), spread, qw, kvw, cache, gatew, upw, outw, downw)


def fits(sizes, rows, seq_dev, d_dev, q_dev, ff_dev, weight_bytes):
    ngx, ngy, ngz = sizes
    heads_dev = q_dev // HEAD_DIM
    return (
        ngx >= 3
        and rows < 8
        and rows == ngy * seq_dev
        and seq_dev <= 4
        and heads_dev in (2, 4, 8)
        and heads_dev * ngy * ngz == HEADS
        and d_dev % 1024 == 0
        and heads_dev % ngx == 0
        and 2 * HEAD_DIM % (ngy * ngz * 128) == 0
        and ff_dev % (ngx * 128) == 0
        and weight_bytes <= 60 * 2**20
    )


def choose(sizes, *args):
    held = sum(a.size * a.dtype.itemsize for a in args[2:9])
    rows, d_dev = args[0].shape
    seq_dev = args[8].shape[0]
    if fits(sizes, rows, seq_dev, d_dev, args[2].shape[1], args[5].shape[1], held):
        return fused(sizes, *args)
    return body(*args)


def solution(mesh):
    sizes = tuple(mesh.shape[a] for a in ("gx", "gy", "gz"))
    chosen = functools.partial(choose, sizes)
    in_specs = (
        P("group", "gx"),
        P("gx"),
        P("gx", ("gy", "gz")),
        P("gx", None),
        P(("gy", "gz"), "gx"),
        P("gx", ("gy", "gz")),
        P("gx", ("gy", "gz")),
        P(("gy", "gz"), "gx"),
        P(("group", "gy"), ("gx", "gz"), None),
        P(("group", "gy")),
    )
    out_specs = (P("group", "gx"), P(("group", "gy"), None))
    return jax.shard_map(chosen, mesh=mesh, in_specs=in_specs, out_specs=out_specs, check_vma=False)
```

```python
import functools
import itertools

import jax
import jax.numpy as jnp
import numpy as np
from jax import lax
from jax.experimental import pallas as pl
from jax.experimental.pallas import tpu as pltpu
from jax.sharding import PartitionSpec as P

D = 8192
HEADS = 16
HEAD_DIM = 256


epsilon = 1e-05
masked_fill = -1e30
rotary_base = 10000.0


def joined(part, axis, combine):
    gathered = jax.tree.map(lambda a: lax.all_gather(a, axis), part)

    def take(source):
        return jax.tree.map(lambda a: lax.dynamic_index_in_dim(a, source, 0, False), gathered)

    return lax.fori_loop(
        1, lax.axis_size(axis), lambda source, state: combine(state, take(source)), take(0)
    )


def rotate(values, angle):
    middle = values.shape[-1] // 2
    first = values[..., :middle]
    second = values[..., middle:]
    cosine = jnp.cos(angle)
    sine_part = jnp.sin(angle)
    return jnp.concatenate(
        [first * cosine - second * sine_part, first * sine_part + second * cosine], -1
    )


def angles(lengths, head_dim):
    middle = head_dim // 2
    spread = rotary_base ** (-jnp.arange(middle, dtype=jnp.float32) / middle)
    return lengths.astype(jnp.float32)[:, None] * spread[None, :]


def combine(earlier, later):
    top = jnp.maximum(earlier[0], later[0])
    first_scale = jnp.exp(earlier[0] - top)
    second_scale = jnp.exp(later[0] - top)
    numer = earlier[1] * first_scale[..., None] + later[1] * second_scale[..., None]
    denom = earlier[2] * first_scale + later[2] * second_scale
    return (top, numer, denom)


def body(
    tokens,
    norm_gain,
    q_weight,
    kv_weight,
    out_weight,
    gate_weight,
    up_weight,
    down_weight,
    kv_cache,
    lengths,
):
    inputs = tokens.astype(jnp.float32)
    totals = lax.psum((jnp.sum(inputs, 1), jnp.sum(inputs * inputs, 1)), "gx")
    center = totals[0] / D
    spread_sq = totals[1] / D - center * center
    normed = (
        (inputs - center[:, None]) * lax.rsqrt(spread_sq + epsilon)[:, None] * norm_gain[None, :]
    ).astype(jnp.bfloat16)
    query_part = jnp.dot(normed, q_weight, preferred_element_type=jnp.float32)
    keyval_part = jnp.dot(normed, kv_weight, preferred_element_type=jnp.float32)
    gate_part = jnp.dot(normed, gate_weight, preferred_element_type=jnp.float32)
    up_part = jnp.dot(normed, up_weight, preferred_element_type=jnp.float32)
    query, keyval, gate, upward = lax.psum((query_part, keyval_part, gate_part, up_part), "gx")
    hidden = (jax.nn.silu(gate) * upward).astype(jnp.bfloat16)
    seq_dev = lengths.shape[0]
    row_groups = lax.axis_size("gy")
    block = q_weight.shape[1]
    first_row = lax.axis_index("gy") * seq_dev
    angle = angles(lengths, HEAD_DIM)
    own_keyval = lax.dynamic_slice_in_dim(keyval, first_row, seq_dev, 0)
    new_kv = jnp.concatenate(
        [rotate(own_keyval[:, :HEAD_DIM], angle), own_keyval[:, HEAD_DIM:]], 1
    ).astype(jnp.bfloat16)
    query_bf = query.astype(jnp.bfloat16)
    every_head = lax.all_gather(query_bf, ("gy", "gz"), axis=1, tiled=True)
    own_query = lax.dynamic_slice_in_dim(every_head, first_row, seq_dev, 0)
    rotated = rotate(
        own_query.astype(jnp.float32).reshape(seq_dev, HEADS, HEAD_DIM), angle[:, None, :]
    ).astype(jnp.bfloat16)
    ctx_dev = kv_cache.shape[1]
    offset = lax.axis_index(("gx", "gz")) * ctx_dev
    positions = offset + jnp.arange(ctx_dev, dtype=jnp.int32)
    live = positions[None, :] < lengths[:, None]
    scale = HEAD_DIM ** (-0.5)
    scores = (
        jnp.einsum(
            "shd,scd->shc", rotated, kv_cache[:, :, :HEAD_DIM], preferred_element_type=jnp.float32
        )
        * scale
    )
    key_new = new_kv[:, :HEAD_DIM]
    value_new = new_kv[:, HEAD_DIM:]
    own_score = (
        jnp.einsum("shd,sd->sh", rotated, key_new, preferred_element_type=jnp.float32) * scale
    )
    hidden_scores = jnp.where(live[:, None, :], scores, masked_fill)
    local_top = jnp.maximum(jnp.max(hidden_scores, 2), own_score)
    weights = jnp.where(live[:, None, :], jnp.exp(hidden_scores - local_top[..., None]), 0.0)
    numer = jnp.einsum(
        "shc,scd->shd",
        weights.astype(jnp.bfloat16),
        kv_cache[:, :, HEAD_DIM:],
        preferred_element_type=jnp.float32,
    )
    denom = jnp.sum(weights, 2)
    top, numer, denom = joined((local_top, numer, denom), ("gx", "gz"), combine)
    own_weight = jnp.exp(own_score - top)
    numer = numer + own_weight[..., None] * value_new.astype(jnp.float32)[:, None, :]
    denom = denom + own_weight
    attended = (numer / denom[..., None]).astype(jnp.bfloat16)
    grouped = attended.reshape(seq_dev, row_groups, HEADS * HEAD_DIM // row_groups)
    picked = lax.dynamic_slice_in_dim(grouped, lax.axis_index("gz") * block, block, 2)
    head_block = lax.all_to_all(picked, "gy", split_axis=1, concat_axis=0, tiled=True).reshape(
        seq_dev * row_groups, block
    )
    partial_value = jnp.dot(head_block, out_weight, preferred_element_type=jnp.float32) + jnp.dot(
        hidden, down_weight, preferred_element_type=jnp.float32
    )
    total = lax.psum(partial_value, ("gy", "gz"))
    mixed = (inputs + total).astype(jnp.bfloat16)
    return (mixed, new_kv)


MESH = pl.DeviceIdType.MESH
F32 = jnp.float32
BF16 = jnp.bfloat16


def kernel(
    dims,
    lengths_h,
    tokens_h,
    gain_h,
    q_h,
    kv_h,
    cache_h,
    gate_h,
    up_h,
    out_h,
    down_h,
    mixed_ref,
    newkv_ref,
    lengths_ref,
    tokens_v,
    gain_v,
    q_v,
    kv_v,
    cache_v,
    gu_v,
    out_v,
    down_v,
    load_sem,
    gu_sem,
    down_sem,
    x_v,
    normed_v,
    stat_v,
    q1_v,
    qr_v,
    rot_v,
    part_v,
    prs_v,
    gsend_v,
    grs_v,
    own_v,
    hid_v,
    acc_v,
    heads_v,
    fin_v,
    send_sem,
    recv_sem,
    h_recv,
    f_recv,
):
    ngx, ngy, ngz, rows, rp = dims
    gx, gy, gz = lax.axis_index("gx"), lax.axis_index("gy"), lax.axis_index("gz")
    dx = x_v.shape[1]
    qd = q_v.shape[1]
    heads_dev = qd // HEAD_DIM
    kw = kv_v.shape[1]
    seq_dev = cache_v.shape[0]
    ctx_dev = cache_v.shape[1]
    fb = gu_v.shape[3]
    owners = ngx * ngz
    spots = ngy * ngz
    pairs = HEADS // 2
    pairs_dev = heads_dev // 2
    slots = rp // 2
    wide = 16 // pairs_dev
    scale = HEAD_DIM ** (-0.5)
    middle = HEAD_DIM // 2
    parts = fin_v.shape[0]
    piece_cols = dx // parts
    me_owner = gx * ngz + gz
    spot = gy * ngz + gz

    def rolled(values, shift, axis):
        shift = shift % values.shape[axis]
        return pltpu.roll(values, shift, axis) if shift else values

    lane = lax.broadcasted_iota(jnp.int32, (rp, 128), 1)
    row = lax.broadcasted_iota(jnp.int32, (rp, 128), 0)
    above = row < slots

    def split_three(values):
        pieces = []
        for c in range(2):
            scaled = values * 65537.0
            pieces.append(scaled - (scaled - values))
            values = values - pieces[-1]
        return jnp.where(lane < 32, pieces[0], jnp.where(lane < 64, pieces[1], values))

    def join_three(pieces):
        pieces = pieces.astype(F32)
        return pieces + rolled(pieces, -32, 1) + rolled(pieces, -64, 1)

    def other(j):
        return jnp.where(gx <= j, j + 1, j)

    def block_at(step):
        if step == ngx - 1:
            return gx
        return jnp.where(gx == ngx - 1, step, other((step + ngx - 2) % (ngx - 1)))

    def source_at(step):
        return gx if step == 0 else other(step - 1)

    def columns_of(block, width):
        return pl.ds(pl.multiple_of(block * width, width), width)

    loads = [
        pltpu.make_async_copy(a, b, load_sem.at[i])
        for i, (a, b) in enumerate(
            (
                (tokens_h, tokens_v),
                (gain_h, gain_v),
                (lengths_h, lengths_ref),
                (kv_h.at[:, columns_of(spot, kw)], kv_v),
                (q_h, q_v),
                (cache_h, cache_v),
                (out_h, out_v),
            )
        )
    ]

    def gu_start(step):
        columns = columns_of(block_at(step), fb)
        pltpu.make_async_copy(gate_h.at[:, columns], gu_v.at[step, 0], gu_sem.at[0, step]).start()
        pltpu.make_async_copy(up_h.at[:, columns], gu_v.at[step, 1], gu_sem.at[1, step]).start()

    def down_copy(step):
        picked = columns_of(source_at(step), fb)
        return pltpu.make_async_copy(down_h.at[picked], down_v.at[step], down_sem.at[step])

    def last_copy(part):
        picked = columns_of(source_at(ngx - 1), fb)
        columns = pl.ds(part * piece_cols, piece_cols)
        return pltpu.make_async_copy(
            down_h.at[picked, columns],
            down_v.at[ngx - 1, :, columns],
            down_sem.at[ngx - 1 + part],
        )

    offsets = [o for o in itertools.product(range(ngx), range(ngy), range(ngz)) if any(o)]

    def shifted(ox, oy, oz):
        return lax.rem(gx + ox, ngx), lax.rem(gy + oy, ngy), lax.rem(gz + oz, ngz)

    def at(px, py, pz):
        return {"gx": px, "gy": py, "gz": pz}

    barrier = pltpu.get_barrier_semaphore()
    for offset in offsets:
        pl.semaphore_signal(barrier, inc=1, device_id=at(*shifted(*offset)), device_id_type=MESH)

    for i in range(5):
        loads[i].start()

    sc0 = jax.named_scope('begin')
    sc0.__enter__()
    loads[0].wait()
    gu_start(0)
    x_v[...] = jnp.zeros_like(x_v)
    x_v[0:rows, :] = tokens_v[...].astype(F32)
    x = x_v[...]
    sums = jnp.sum(x, 1, keepdims=True)
    stat = jnp.where(lane % 32 < 16, sums, jnp.sum(x * x, 1, keepdims=True))
    stat = split_three(stat).astype(BF16)
    loads[1].wait()
    gu_start(1)
    spare = lax.broadcasted_iota(jnp.int32, (rp, dx), 0) == rows
    centred = jnp.where(spare, 1.0, x - sums / dx)
    normed_v[...] = (centred * gain_v[...]).astype(BF16)

    loads[2].wait()
    loads[5].start()
    line = lax.rem(lax.broadcasted_iota(jnp.int32, (rp, middle), 0), slots)
    length = jnp.zeros((rp, middle), jnp.int32)
    for s in range(seq_dev):
        length = jnp.where(line == s, lengths_ref[s], length)
    place = lax.broadcasted_iota(jnp.int32, (rp, middle), 1).astype(F32)
    angle = length.astype(F32) * jnp.exp(place * (-np.log(rotary_base) / middle))
    cosine = jnp.cos(angle)
    sine = jnp.sin(angle)

    sc0.__exit__(None, None, None)
    sc0 = jax.named_scope('qdot')
    sc0.__enter__()
    loads[3].wait()
    gu_start(2)
    kv_part = jnp.dot(normed_v[...], kv_v[...], preferred_element_type=F32)
    loads[4].wait()
    for step in range(3, ngx):
        gu_start(step)
    q_part = jnp.dot(normed_v[...], q_v[...], preferred_element_type=F32)
    stat_v[gx] = stat
    for y in range(ngy):
        for h in range(heads_dev + 1):
            a = q_part[:, h * HEAD_DIM : h * HEAD_DIM + middle] if h < heads_dev else kv_part
            b = q_part[:, h * HEAD_DIM + middle : (h + 1) * HEAD_DIM] if h < heads_dev else a
            tile = jnp.where(above, rolled(a, -y * seq_dev, 0), rolled(b, slots - y * seq_dev, 0))
            tile = jnp.where(row == slots - 1, a[rows : rows + 1, :], tile)
            tile = jnp.where(row == rp - 1, b[rows : rows + 1, :], tile)
            q1_v[y, h] = tile.astype(BF16)

    sc0.__exit__(None, None, None)
    with jax.named_scope('barrier'):
        pl.semaphore_wait(barrier, len(offsets))

    def send(source, target, sends, receives, device):
        pltpu.make_async_remote_copy(
            src_ref=source,
            dst_ref=target,
            send_sem=sends,
            recv_sem=receives,
            device_id=device,
            device_id_type=MESH,
        ).start()

    def arrival(slot, semaphore):
        return pltpu.make_async_remote_copy(
            src_ref=slot,
            dst_ref=slot,
            send_sem=semaphore,
            recv_sem=semaphore,
            device_id=at(gx, gy, gz),
            device_id_type=MESH,
        )

    def arrived(slot, semaphore):
        arrival(slot, semaphore).wait_recv()

    def left(slot, semaphore):
        arrival(slot, semaphore).wait_send()

    for j in range(ngx - 1):
        peer = at(other(j), gy, gz)
        send(stat_v.at[gx], stat_v.at[gx], send_sem.at[2], recv_sem.at[2], peer)
    for offset in offsets:
        px, py, pz = shifted(*offset)
        send(
            q1_v.at[py],
            qr_v.at[gx * spots + spot],
            send_sem.at[0],
            recv_sem.at[0],
            at(px, py, pz),
        )
    qr_v[gx * spots + spot] = q1_v[gy]

    def later_loads(k):
        if k == 0:
            down_copy(0).start()
        elif k == 1:
            loads[6].start()
        elif k < ngx:
            down_copy(k - 1).start()
        elif k < 2 * ngx - 1:
            for part in range(parts * (k - ngx) // (ngx - 1), parts * (k - ngx + 1) // (ngx - 1)):
                last_copy(part).start()

    def gate_up(step):
        for which in range(2):
            slot = gu_v.at[step, which]
            pltpu.make_async_copy(slot, slot, gu_sem.at[which, step]).wait()
            later_loads(2 * step + which)
            part = jnp.dot(normed_v[...], gu_v[step, which], preferred_element_type=F32)
            if step < ngx - 1:
                gsend_v[step, which] = part.astype(BF16)
            else:
                own_v[which] = part
        if step < ngx - 1:
            send(
                gsend_v.at[step],
                grs_v.at[gx],
                send_sem.at[1],
                recv_sem.at[1],
                at(block_at(step), gy, gz),
            )

    def moments():
        arrived(stat_v.at[pl.ds(0, ngx - 1)], recv_sem.at[2])
        stats = [join_three(stat_v[k]) for k in range(ngx)]
        totals = functools.reduce(jnp.add, stats)
        center = totals[:, 0:1] / D
        spread_sq = totals[:, 16:17] / D - center * center
        drift = [part[:, 0:1] / dx - center for part in stats]
        return drift, lax.rsqrt(spread_sq + epsilon)

    def packed(column):
        values = jnp.broadcast_to(column, (rp, 128))
        result = None
        for y in range(ngy):
            upper = rolled(values, -y * seq_dev, 0)
            lower = rolled(values, slots - y * seq_dev, 0)
            choice = jnp.where(above, upper, lower)
            result = choice if result is None else jnp.where(gy == y, choice, result)
        return result

    fold = pairs_dev * (HEAD_DIM // 128) == slots and seq_dev == slots - 1
    base = pairs_dev * (HEAD_DIM // 128) - fold

    def folded(tiles, t):
        if not fold:
            return tiles[t]
        return jnp.where(row % slots == slots - 1, rolled(tiles[-1], slots - 1 - t, 0), tiles[t])

    def unfolded(tiles):
        if not fold:
            return tiles
        last = rolled(tiles[0], 1 - slots, 0)
        for t in range(1, base):
            last = jnp.where(row % slots == t, rolled(tiles[t], t + 1 - slots, 0), last)
        return tiles + [last]

    def attend():
        drifts = [packed(column) for column in drift]
        factor = packed(inverse)

        def summed(place, h):
            total = None
            for k in range(ngx):
                tile = qr_v[k * spots + place, h].astype(F32)
                gain = jnp.where(above, tile[slots - 1 : slots, :], tile[rp - 1 : rp, :])
                tile = tile + drifts[k] * gain
                total = tile if total is None else total + tile
            return total * factor

        arrived(qr_v.at[pl.ds(0, ngx * spots - 1)], recv_sem.at[0])
        kv_tiles = [summed(place, heads_dev) for place in range(spots)]
        keyval = jnp.concatenate(kv_tiles, 1)
        a = keyval[:, :middle]
        b = keyval[:, middle:HEAD_DIM]
        newkv = jnp.concatenate(
            [a * cosine - b * sine, a * sine + b * cosine, keyval[:, HEAD_DIM:]], 1
        ).astype(BF16)
        newkv_ref[...] = newkv[:seq_dev]
        newkv = newkv.astype(F32)
        owns = []
        for p in range(pairs):
            place, h = 2 * p // heads_dev, 2 * p % heads_dev
            even = summed(place, h).astype(BF16).astype(F32)
            odd = summed(place, h + 1).astype(BF16).astype(F32)
            a = jnp.where(above, even, rolled(odd, slots, 0))
            b = jnp.where(above, rolled(even, slots, 0), odd)
            first = (a * cosine - b * sine).astype(BF16).astype(F32)
            second = (a * sine + b * cosine).astype(BF16).astype(F32)
            rot_v[p, :, :middle] = first
            rot_v[p, :, middle:] = second
            product = first * newkv[:, :middle] + second * newkv[:, middle:HEAD_DIM]
            owns.append(jnp.sum(product, 1, keepdims=True) * scale)
        count = pairs * rp
        rotated = rot_v[...].reshape(count, HEAD_DIM).astype(BF16)
        own = jnp.where(me_owner == 0, jnp.concatenate(owns, 0), masked_fill)
        line = lax.rem(lax.broadcasted_iota(jnp.int32, (count, ctx_dev), 0), slots)
        position = me_owner * ctx_dev + lax.broadcasted_iota(jnp.int32, (count, ctx_dev), 1)
        scores = jnp.full((count, ctx_dev), masked_fill, F32)
        limit = jnp.zeros((count, ctx_dev), jnp.int32)
        loads[5].wait()
        for s in range(seq_dev):
            raw = lax.dot_general(
                rotated,
                cache_v[s, :, :HEAD_DIM],
                (((1,), (1,)), ((), ())),
                preferred_element_type=F32,
            )
            limit = jnp.where(line == s, lengths_ref[s], limit)
            scores = jnp.where(line == s, raw * scale, scores)
        live = position < limit
        scores = jnp.where(live, scores, masked_fill)
        top = jnp.maximum(jnp.max(scores, 1, keepdims=True), own)
        weights = jnp.where(live, jnp.exp(scores - top), 0.0)
        own_weight = jnp.where(me_owner == 0, jnp.exp(own - top), 0.0)
        denom = jnp.sum(weights, 1, keepdims=True) + own_weight
        value = newkv[:, HEAD_DIM:]
        numer = own_weight * jnp.concatenate([value] * pairs, 0)
        for s in range(seq_dev):
            numer = numer + jnp.dot(
                jnp.where(line == s, weights, 0.0).astype(BF16),
                cache_v[s, :, HEAD_DIM:],
                preferred_element_type=F32,
            )
        for d in range(spots):
            side = jnp.zeros((rp, 128), F32)
            tiles = []
            for j in range(pairs_dev):
                low = (d * pairs_dev + j) * rp
                for c in range(HEAD_DIM // 128):
                    tiles.append(numer[low : low + rp, c * 128 : (c + 1) * 128])
                inner = lane % 32
                side = jnp.where((inner >= j * wide) & (inner < 16), top[low : low + rp], side)
                side = jnp.where(inner >= 16 + j * wide, denom[low : low + rp], side)
            for t in range(base):
                part_v[d, t] = folded(tiles, t).astype(BF16)
            part_v[d, base] = split_three(side).astype(BF16)
        mine = gy * owners + me_owner
        for offset in offsets:
            px, py, pz = shifted(*offset)
            send(
                part_v.at[py * ngz + pz],
                prs_v.at[mine],
                send_sem.at[3],
                recv_sem.at[3],
                at(px, py, pz),
            )
        prs_v[mine] = part_v[spot]

    def combine_parts():
        arrived(prs_v.at[pl.ds(0, ngy * owners - 1)], recv_sem.at[3])
        groups = []
        for y in range(ngy):
            sides = []
            for o in range(owners):
                k = y * owners + o
                sides.append(join_three(prs_v[k, base]))
            top = functools.reduce(jnp.maximum, sides)
            factors = [jnp.where(lane < 16, jnp.exp(side - top), 0.0) for side in sides]
            denom = functools.reduce(
                jnp.add, [rolled(f, 16, 1) * side for f, side in zip(factors, sides)]
            )
            share = rolled(1.0 / denom, -16, 1)
            factors = [f * share for f in factors]
            tiles = [None] * (base + fold)
            for o in range(owners):
                pieces = unfolded([prs_v[y * owners + o, t].astype(F32) for t in range(base)])
                for j in range(pairs_dev):
                    f = factors[o][:, j * wide : j * wide + 1]
                    for c in range(HEAD_DIM // 128):
                        t = j * (HEAD_DIM // 128) + c
                        piece = f * pieces[t]
                        tiles[t] = piece if tiles[t] is None else tiles[t] + piece
            groups.append(tiles)
        for h in range(heads_dev):
            for c in range(HEAD_DIM // 128):
                total = jnp.zeros((rp, 128), F32)
                for y in range(ngy):
                    tile = groups[y][(h // 2) * (HEAD_DIM // 128) + c]
                    moved = rolled(tile, y * seq_dev - (h % 2) * slots, 0)
                    inside = (row >= y * seq_dev) & (row < (y + 1) * seq_dev)
                    total = jnp.where(inside, moved, total)
                low = h * HEAD_DIM + c * 128
                heads_v[:, low : low + 128] = total.astype(BF16)

    def hidden():
        arrived(grs_v.at[pl.ds(0, ngx - 1)], recv_sem.at[1])
        g = own_v[0]
        u = own_v[1]
        mean_drift = jnp.zeros((rp, 1), F32)
        for k in range(ngx):
            mean_drift = jnp.where(gx == k, drift[k], mean_drift)
        g = g + mean_drift * g[rows : rows + 1, :]
        u = u + mean_drift * u[rows : rows + 1, :]
        for j in range(ngx - 1):
            peer = other(j)
            shift = jnp.where(gx <= j, drift[j + 1], drift[j])
            g_part = grs_v[peer, 0].astype(F32)
            u_part = grs_v[peer, 1].astype(F32)
            g = g + g_part + shift * g_part[rows : rows + 1, :]
            u = u + u_part + shift * u_part[rows : rows + 1, :]
        g = g * inverse
        u = u * inverse
        hid_v[gx] = (g / (1.0 + jnp.exp(-g)) * u).astype(BF16)
        for j in range(ngx - 1):
            send(hid_v.at[gx], hid_v.at[gx], send_sem.at[4], h_recv.at[gx], at(other(j), gy, gz))

    def down_product(step):
        source = source_at(step)
        if step:
            arrived(hid_v.at[source], h_recv.at[source])
        down_copy(step).wait()
        product = jnp.dot(hid_v[source], down_v[step], preferred_element_type=F32)
        if step:
            acc_v[...] += product
        else:
            acc_v[...] = product

    peers = [o for o in itertools.product(range(ngy), range(ngz)) if any(o)]

    def scoped(name, f, *args):
        with jax.named_scope(name):
            return f(*args)

    scoped("gu0", gate_up, 0)
    for step in range(1, ngx - 1):
        scoped("gu%d" % step, gate_up, step)
    drift, inverse = scoped("moments", moments)
    scoped("attend", attend)
    scoped("gulast", gate_up, ngx - 1)
    scoped("hidden", hidden)
    scoped("down0", down_product, 0)
    scoped("combine", combine_parts)

    def out_product():
        loads[6].wait()
        acc_v[...] += jnp.dot(heads_v[...], out_v[...], preferred_element_type=F32)

    scoped("outp", out_product)
    for step in range(1, ngx - 1):
        scoped("down%d" % step, down_product, step)

    def last_down():
        source = source_at(ngx - 1)
        arrived(hid_v.at[source], h_recv.at[source])
        for part in range(parts):
            columns = slice(part * piece_cols, (part + 1) * piece_cols)
            last_copy(part).wait()
            total = acc_v[:, columns] + jnp.dot(
                hid_v[source], down_v[ngx - 1, :, columns], preferred_element_type=F32
            )
            fin_v[part, spot] = total.astype(BF16)
            for oy, oz in peers:
                px, py, pz = shifted(0, oy, oz)
                send(
                    fin_v.at[part, spot],
                    fin_v.at[part, spot],
                    send_sem.at[5],
                    f_recv.at[part],
                    at(px, py, pz),
                )
            acc_v[:, columns] = total

    scoped("lastdown", last_down)

    def final():
        for part in range(parts):
            columns = slice(part * piece_cols, (part + 1) * piece_cols)
            total = x_v[:, columns] + acc_v[:, columns]
            arrived(fin_v.at[part, pl.ds(0, spots - 1)], f_recv.at[part])
            for oy, oz in peers:
                px, py, pz = shifted(0, oy, oz)
                total = total + fin_v[part, py * ngz + pz].astype(F32)
            mixed_ref[:, columns] = total[:rows].astype(BF16)

    scoped("final", final)

    def drain():
        left(qr_v.at[pl.ds(0, ngx * spots - 1)], send_sem.at[0])
        left(gsend_v, send_sem.at[1])
        left(stat_v.at[pl.ds(0, ngx - 1)], send_sem.at[2])
        left(prs_v.at[pl.ds(0, ngy * owners - 1)], send_sem.at[3])
        left(hid_v.at[pl.ds(0, ngx - 1)], send_sem.at[4])
        left(fin_v.at[:, pl.ds(0, spots - 1)], send_sem.at[5])

    scoped("drain", drain)


def write_out(mixed_v, newkv_v, mixed_h, newkv_h, sem):
    first = pltpu.make_async_copy(mixed_v, mixed_h, sem.at[0])
    second = pltpu.make_async_copy(newkv_v, newkv_h, sem.at[1])
    first.start()
    second.start()
    first.wait()
    second.wait()


def fused(sizes, *args):
    (tokens, gain, qw, kvw, outw, gatew, upw, downw, cache, lengths) = args
    ngx, ngy, ngz = sizes
    rows, dx = tokens.shape
    rp = (rows // 8 + 1) * 8
    qd = qw.shape[1]
    fb = gatew.shape[1] // ngx
    heads_dev = qd // HEAD_DIM
    owners = ngx * ngz
    spots = ngy * ngz
    kw = kvw.shape[1] // spots
    middle = HEAD_DIM // 2
    slots = rp // 2
    tiles = heads_dev // 2 * (HEAD_DIM // 128)
    fold = tiles == slots and cache.shape[0] == slots - 1
    tiles = tiles - fold + 1
    dma = pltpu.SemaphoreType.DMA
    vm = pltpu.VMEM
    scratch = [
        pltpu.SMEM(lengths.shape, jnp.int32),
        vm(tokens.shape, BF16),
        vm((1, dx), F32),
        vm(qw.shape, BF16),
        vm((dx, kw), BF16),
        vm(cache.shape, BF16),
        vm((ngx, 2, dx, fb), BF16),
        vm(outw.shape, BF16),
        vm((ngx, fb, dx), BF16),
        dma((7,)),
        dma((2, ngx)),
        dma((ngx + 1,)),
        vm((rp, dx), F32),
        vm((rp, dx), BF16),
        vm((ngx, rp, 128), BF16),
        vm((ngy, heads_dev + 1, rp, 128), BF16),
        vm((ngx * spots, heads_dev + 1, rp, 128), BF16),
        vm((HEADS // 2, rp, HEAD_DIM), F32),
        vm((spots, tiles, rp, 128), BF16),
        vm((ngy * owners, tiles, rp, 128), BF16),
        vm((ngx - 1, 2, rp, fb), BF16),
        vm((ngx, 2, rp, fb), BF16),
        vm((2, rp, fb), F32),
        vm((ngx, rp, fb), BF16),
        vm((rp, dx), F32),
        vm((rp, qd), BF16),
        vm((2, spots, rp, dx // 2), BF16),
        dma((6,)),
        dma((4,)),
        dma((ngx,)),
        dma((2,)),
    ]
    anywhere = pl.BlockSpec(memory_space=pl.ANY)
    results = pl.pallas_call(
        functools.partial(kernel, (ngx, ngy, ngz, rows, rp)),
        out_shape=(
            pltpu.VMEM(tokens.shape, BF16),
            pltpu.VMEM((cache.shape[0], 2 * HEAD_DIM), BF16),
        ),
        in_specs=[anywhere] * 10,
        out_specs=(pl.BlockSpec(memory_space=pltpu.VMEM),) * 2,
        scratch_shapes=scratch,
        compiler_params=pltpu.CompilerParams(
            collective_id=0, has_side_effects=True, vmem_limit_bytes=61 * 2**20
        ),
    )(lengths, tokens, gain.reshape(1, dx), qw, kvw, cache, gatew, upw, outw, downw)
    results = [pltpu.with_memory_space_constraint(a, vm) for a in results]
    return pl.pallas_call(
        write_out,
        out_shape=tuple(pltpu.HBM(a.shape, a.dtype) for a in results),
        in_specs=[pl.BlockSpec(memory_space=vm)] * 2,
        out_specs=(pl.BlockSpec(memory_space=pltpu.HBM),) * 2,
        scratch_shapes=[dma((2,))],
    )(*results)


def fits(sizes, rows, seq_dev, d_dev, q_dev, ff_dev, weight_bytes):
    ngx, ngy, ngz = sizes
    heads_dev = q_dev // HEAD_DIM
    return (
        ngx >= 3
        and rows < 8
        and rows == ngy * seq_dev
        and seq_dev <= 3
        and heads_dev in (2, 4, 8)
        and heads_dev * ngy * ngz == HEADS
        and d_dev % 1024 == 0
        and 2 * HEAD_DIM == ngy * ngz * 128
        and ff_dev % (ngx * 128) == 0
        and weight_bytes <= 60 * 2**20
    )


def choose(sizes, *args):
    held = sum(a.size * a.dtype.itemsize for a in args[2:9])
    rows, d_dev = args[0].shape
    seq_dev = args[8].shape[0]
    if fits(sizes, rows, seq_dev, d_dev, args[2].shape[1], args[5].shape[1], held):
        return fused(sizes, *args)
    return body(*args)


def solution(mesh):
    sizes = tuple(mesh.shape[a] for a in ("gx", "gy", "gz"))
    chosen = functools.partial(choose, sizes)
    in_specs = (
        P("group", "gx"),
        P("gx"),
        P("gx", ("gy", "gz")),
        P("gx", None),
        P(("gy", "gz"), "gx"),
        P("gx", ("gy", "gz")),
        P("gx", ("gy", "gz")),
        P(("gy", "gz"), "gx"),
        P(("group", "gy"), ("gx", "gz"), None),
        P(("group", "gy")),
    )
    out_specs = (P("group", "gx"), P(("group", "gy"), None))
    return jax.shard_map(chosen, mesh=mesh, in_specs=in_specs, out_specs=out_specs, check_vma=False)
```

```python
import functools
import itertools

import jax
import jax.numpy as jnp
import numpy as np
from jax import lax
from jax.experimental import pallas as pl
from jax.experimental.pallas import tpu as pltpu
from jax.sharding import PartitionSpec as P

D = 8192
HEADS = 16
HEAD_DIM = 256


epsilon = 1e-05
masked_fill = -1e30
rotary_base = 10000.0


def joined(part, axis, combine):
    gathered = jax.tree.map(lambda a: lax.all_gather(a, axis), part)

    def take(source):
        return jax.tree.map(lambda a: lax.dynamic_index_in_dim(a, source, 0, False), gathered)

    return lax.fori_loop(
        1, lax.axis_size(axis), lambda source, state: combine(state, take(source)), take(0)
    )


def rotate(values, angle):
    middle = values.shape[-1] // 2
    first = values[..., :middle]
    second = values[..., middle:]
    cosine = jnp.cos(angle)
    sine_part = jnp.sin(angle)
    return jnp.concatenate(
        [first * cosine - second * sine_part, first * sine_part + second * cosine], -1
    )


def angles(lengths, head_dim):
    middle = head_dim // 2
    spread = rotary_base ** (-jnp.arange(middle, dtype=jnp.float32) / middle)
    return lengths.astype(jnp.float32)[:, None] * spread[None, :]


def combine(earlier, later):
    top = jnp.maximum(earlier[0], later[0])
    first_scale = jnp.exp(earlier[0] - top)
    second_scale = jnp.exp(later[0] - top)
    numer = earlier[1] * first_scale[..., None] + later[1] * second_scale[..., None]
    denom = earlier[2] * first_scale + later[2] * second_scale
    return (top, numer, denom)


def body(
    tokens,
    norm_gain,
    q_weight,
    kv_weight,
    out_weight,
    gate_weight,
    up_weight,
    down_weight,
    kv_cache,
    lengths,
):
    inputs = tokens.astype(jnp.float32)
    totals = lax.psum((jnp.sum(inputs, 1), jnp.sum(inputs * inputs, 1)), "gx")
    center = totals[0] / D
    spread_sq = totals[1] / D - center * center
    normed = (
        (inputs - center[:, None]) * lax.rsqrt(spread_sq + epsilon)[:, None] * norm_gain[None, :]
    ).astype(jnp.bfloat16)
    query_part = jnp.dot(normed, q_weight, preferred_element_type=jnp.float32)
    keyval_part = jnp.dot(normed, kv_weight, preferred_element_type=jnp.float32)
    gate_part = jnp.dot(normed, gate_weight, preferred_element_type=jnp.float32)
    up_part = jnp.dot(normed, up_weight, preferred_element_type=jnp.float32)
    query, keyval, gate, upward = lax.psum((query_part, keyval_part, gate_part, up_part), "gx")
    hidden = (jax.nn.silu(gate) * upward).astype(jnp.bfloat16)
    seq_dev = lengths.shape[0]
    row_groups = lax.axis_size("gy")
    block = q_weight.shape[1]
    first_row = lax.axis_index("gy") * seq_dev
    angle = angles(lengths, HEAD_DIM)
    own_keyval = lax.dynamic_slice_in_dim(keyval, first_row, seq_dev, 0)
    new_kv = jnp.concatenate(
        [rotate(own_keyval[:, :HEAD_DIM], angle), own_keyval[:, HEAD_DIM:]], 1
    ).astype(jnp.bfloat16)
    query_bf = query.astype(jnp.bfloat16)
    every_head = lax.all_gather(query_bf, ("gy", "gz"), axis=1, tiled=True)
    own_query = lax.dynamic_slice_in_dim(every_head, first_row, seq_dev, 0)
    rotated = rotate(
        own_query.astype(jnp.float32).reshape(seq_dev, HEADS, HEAD_DIM), angle[:, None, :]
    ).astype(jnp.bfloat16)
    ctx_dev = kv_cache.shape[1]
    offset = lax.axis_index(("gx", "gz")) * ctx_dev
    positions = offset + jnp.arange(ctx_dev, dtype=jnp.int32)
    live = positions[None, :] < lengths[:, None]
    scale = HEAD_DIM ** (-0.5)
    scores = (
        jnp.einsum(
            "shd,scd->shc", rotated, kv_cache[:, :, :HEAD_DIM], preferred_element_type=jnp.float32
        )
        * scale
    )
    key_new = new_kv[:, :HEAD_DIM]
    value_new = new_kv[:, HEAD_DIM:]
    own_score = (
        jnp.einsum("shd,sd->sh", rotated, key_new, preferred_element_type=jnp.float32) * scale
    )
    hidden_scores = jnp.where(live[:, None, :], scores, masked_fill)
    local_top = jnp.maximum(jnp.max(hidden_scores, 2), own_score)
    weights = jnp.where(live[:, None, :], jnp.exp(hidden_scores - local_top[..., None]), 0.0)
    numer = jnp.einsum(
        "shc,scd->shd",
        weights.astype(jnp.bfloat16),
        kv_cache[:, :, HEAD_DIM:],
        preferred_element_type=jnp.float32,
    )
    denom = jnp.sum(weights, 2)
    top, numer, denom = joined((local_top, numer, denom), ("gx", "gz"), combine)
    own_weight = jnp.exp(own_score - top)
    numer = numer + own_weight[..., None] * value_new.astype(jnp.float32)[:, None, :]
    denom = denom + own_weight
    attended = (numer / denom[..., None]).astype(jnp.bfloat16)
    grouped = attended.reshape(seq_dev, row_groups, HEADS * HEAD_DIM // row_groups)
    picked = lax.dynamic_slice_in_dim(grouped, lax.axis_index("gz") * block, block, 2)
    head_block = lax.all_to_all(picked, "gy", split_axis=1, concat_axis=0, tiled=True).reshape(
        seq_dev * row_groups, block
    )
    partial_value = jnp.dot(head_block, out_weight, preferred_element_type=jnp.float32) + jnp.dot(
        hidden, down_weight, preferred_element_type=jnp.float32
    )
    total = lax.psum(partial_value, ("gy", "gz"))
    mixed = (inputs + total).astype(jnp.bfloat16)
    return (mixed, new_kv)


MESH = pl.DeviceIdType.MESH
F32 = jnp.float32
BF16 = jnp.bfloat16


def kernel(
    dims,
    lengths_h,
    tokens_h,
    gain_h,
    q_h,
    kv_h,
    cache_h,
    gate_h,
    up_h,
    out_h,
    down_h,
    mixed_ref,
    newkv_ref,
    lengths_ref,
    tokens_v,
    gain_v,
    q_v,
    kv_v,
    cache_v,
    gu_v,
    out_v,
    down_v,
    load_sem,
    gu_sem,
    x_v,
    normed_v,
    stat_v,
    q1_v,
    qr_v,
    rot_v,
    part_v,
    prs_v,
    gsend_v,
    grs_v,
    own_v,
    hid_v,
    acc_v,
    heads_v,
    fin_v,
    send_sem,
    recv_sem,
    h_recv,
    f_recv,
):
    ngx, ngy, ngz, rows, rp = dims
    gx, gy, gz = lax.axis_index("gx"), lax.axis_index("gy"), lax.axis_index("gz")
    dx = x_v.shape[1]
    qd = q_v.shape[1]
    heads_dev = qd // HEAD_DIM
    kw = kv_v.shape[1]
    seq_dev = cache_v.shape[0]
    ctx_dev = cache_v.shape[1]
    fb = gu_v.shape[3]
    owners = ngx * ngz
    spots = ngy * ngz
    pairs = HEADS // 2
    pairs_dev = heads_dev // 2
    slots = rp // 2
    wide = 16 // pairs_dev
    scale = HEAD_DIM ** (-0.5)
    middle = HEAD_DIM // 2
    parts = fin_v.shape[0]
    piece_cols = dx // parts
    me_owner = gx * ngz + gz
    spot = gy * ngz + gz

    def rolled(values, shift, axis):
        shift = shift % values.shape[axis]
        return pltpu.roll(values, shift, axis) if shift else values

    lane = lax.broadcasted_iota(jnp.int32, (rp, 128), 1)
    row = lax.broadcasted_iota(jnp.int32, (rp, 128), 0)
    above = row < slots

    def split_three(values):
        pieces = []
        for c in range(2):
            scaled = values * 65537.0
            pieces.append(scaled - (scaled - values))
            values = values - pieces[-1]
        return jnp.where(lane < 32, pieces[0], jnp.where(lane < 64, pieces[1], values))

    def join_three(pieces):
        pieces = pieces.astype(F32)
        return pieces + rolled(pieces, -32, 1) + rolled(pieces, -64, 1)

    def other(j):
        return jnp.where(gx <= j, j + 1, j)

    def partner(mask):
        result = gx
        for g in range(ngx):
            result = jnp.where(gx == g, g ^ mask, result)
        return result

    def block_at(step):
        if step == ngx - 1:
            return gx
        return partner(ngx - 1 - step)

    def source_at(step):
        return gx if step == 0 else other(step - 1)

    def columns_of(block, width):
        return pl.ds(pl.multiple_of(block * width, width), width)

    loads = [
        pltpu.make_async_copy(a, b, load_sem.at[i])
        for i, (a, b) in enumerate(
            (
                (tokens_h, tokens_v),
                (gain_h, gain_v),
                (lengths_h, lengths_ref),
                (kv_h.at[:, columns_of(spot, kw)], kv_v),
                (q_h, q_v),
                (cache_h, cache_v),
            )
        )
    ]

    def gu_start(step):
        columns = columns_of(block_at(step), fb)
        pltpu.make_async_copy(gate_h.at[:, columns], gu_v.at[step, 0], gu_sem.at[0, step]).start()
        pltpu.make_async_copy(up_h.at[:, columns], gu_v.at[step, 1], gu_sem.at[1, step]).start()

    def again(k):
        return gu_sem.at[k % 2, k // 2]

    out_copy = pltpu.make_async_copy(out_h, out_v, again(1))

    def down_copy(step):
        picked = columns_of(source_at(step), fb)
        return pltpu.make_async_copy(down_h.at[picked], down_v.at[step], again(step + (step > 0)))

    def last_copy(part):
        picked = columns_of(source_at(ngx - 1), fb)
        columns = pl.ds(part * piece_cols, piece_cols)
        return pltpu.make_async_copy(
            down_h.at[picked, columns],
            down_v.at[ngx - 1, :, columns],
            again(ngx + part),
        )

    offsets = [o for o in itertools.product(range(ngx), range(ngy), range(ngz)) if any(o)]

    def shifted(ox, oy, oz):
        return lax.rem(gx + ox, ngx), lax.rem(gy + oy, ngy), lax.rem(gz + oz, ngz)

    def at(px, py, pz):
        return {"gx": px, "gy": py, "gz": pz}

    for i in range(5):
        loads[i].start()

    barrier = pltpu.get_barrier_semaphore()
    for offset in offsets:
        pl.semaphore_signal(barrier, inc=1, device_id=at(*shifted(*offset)), device_id_type=MESH)

    loads[0].wait()
    gu_start(0)
    x_v[...] = jnp.zeros_like(x_v)
    x_v[0:rows, :] = tokens_v[...].astype(F32)
    x = x_v[...]
    sums = jnp.sum(x, 1, keepdims=True)
    stat = jnp.where(lane % 32 < 16, sums, jnp.sum(x * x, 1, keepdims=True))
    stat = split_three(stat).astype(BF16)
    loads[1].wait()
    gu_start(1)
    spare = lax.broadcasted_iota(jnp.int32, (rp, dx), 0) == rows
    centred = jnp.where(spare, 1.0, x - sums / dx)
    normed_v[...] = (centred * gain_v[...]).astype(BF16)

    loads[2].wait()
    loads[5].start()
    line = lax.rem(lax.broadcasted_iota(jnp.int32, (rp, middle), 0), slots)
    length = jnp.zeros((rp, middle), jnp.int32)
    for s in range(seq_dev):
        length = jnp.where(line == s, lengths_ref[s], length)
    place = lax.broadcasted_iota(jnp.int32, (rp, middle), 1).astype(F32)
    angle = length.astype(F32) * jnp.exp(place * (-np.log(rotary_base) / middle))
    cosine = jnp.cos(angle)
    sine = jnp.sin(angle)

    loads[3].wait()
    gu_start(2)
    kv_part = jnp.dot(normed_v[...], kv_v[...], preferred_element_type=F32)
    loads[4].wait()
    for step in range(3, ngx):
        gu_start(step)
    q_part = jnp.dot(normed_v[...], q_v[...], preferred_element_type=F32)
    stat_v[gx] = stat
    for y in range(ngy):
        for h in range(heads_dev + 1):
            a = q_part[:, h * HEAD_DIM : h * HEAD_DIM + middle] if h < heads_dev else kv_part
            b = q_part[:, h * HEAD_DIM + middle : (h + 1) * HEAD_DIM] if h < heads_dev else a
            tile = jnp.where(above, rolled(a, -y * seq_dev, 0), rolled(b, slots - y * seq_dev, 0))
            tile = jnp.where(row == slots - 1, a[rows : rows + 1, :], tile)
            tile = jnp.where(row == rp - 1, b[rows : rows + 1, :], tile)
            q1_v[y, h] = tile.astype(BF16)

    pl.semaphore_wait(barrier, len(offsets))

    def send(source, target, sends, receives, device):
        pltpu.make_async_remote_copy(
            src_ref=source,
            dst_ref=target,
            send_sem=sends,
            recv_sem=receives,
            device_id=device,
            device_id_type=MESH,
        ).start()

    def arrival(slot, semaphore):
        return pltpu.make_async_remote_copy(
            src_ref=slot,
            dst_ref=slot,
            send_sem=semaphore,
            recv_sem=semaphore,
            device_id=at(gx, gy, gz),
            device_id_type=MESH,
        )

    def arrived(slot, semaphore):
        arrival(slot, semaphore).wait_recv()

    def left(slot, semaphore):
        arrival(slot, semaphore).wait_send()

    for j in range(ngx - 1):
        peer = at(other(j), gy, gz)
        send(stat_v.at[gx], stat_v.at[gx], send_sem.at[2], recv_sem.at[2], peer)
    for offset in offsets:
        px, py, pz = shifted(*offset)
        send(
            q1_v.at[py],
            qr_v.at[gx * spots + spot],
            send_sem.at[0],
            recv_sem.at[0],
            at(px, py, pz),
        )
    qr_v[gx * spots + spot] = q1_v[gy]

    def later_loads(k):
        if k == 0:
            down_copy(0).start()
        elif k == 1:
            out_copy.start()
        elif k < ngx:
            down_copy(k - 1).start()
        elif k < ngx + parts:
            last_copy(k - ngx).start()

    def gate_up(step):
        for which in range(2):
            slot = gu_v.at[step, which]
            pltpu.make_async_copy(slot, slot, gu_sem.at[which, step]).wait()
            later_loads(2 * step + which)
            part = jnp.dot(normed_v[...], gu_v[step, which], preferred_element_type=F32)
            if step < ngx - 1:
                gsend_v[step, which] = part.astype(BF16)
            else:
                own_v[which] = part
        if step < ngx - 1:
            send(
                gsend_v.at[step],
                grs_v.at[gx],
                send_sem.at[1],
                recv_sem.at[1],
                at(block_at(step), gy, gz),
            )

    def moments():
        arrived(stat_v.at[pl.ds(0, ngx - 1)], recv_sem.at[2])
        stats = [join_three(stat_v[k]) for k in range(ngx)]
        totals = functools.reduce(jnp.add, stats)
        center = totals[:, 0:1] / D
        spread_sq = totals[:, 16:17] / D - center * center
        drift = [part[:, 0:1] / dx - center for part in stats]
        return drift, lax.rsqrt(spread_sq + epsilon)

    def packed(column):
        values = jnp.broadcast_to(column, (rp, 128))
        result = None
        for y in range(ngy):
            upper = rolled(values, -y * seq_dev, 0)
            lower = rolled(values, slots - y * seq_dev, 0)
            choice = jnp.where(above, upper, lower)
            result = choice if result is None else jnp.where(gy == y, choice, result)
        return result

    fold = pairs_dev * (HEAD_DIM // 128) == slots and seq_dev == slots - 1
    base = pairs_dev * (HEAD_DIM // 128) - fold

    def folded(tiles, t):
        if not fold:
            return tiles[t]
        return jnp.where(row % slots == slots - 1, rolled(tiles[-1], slots - 1 - t, 0), tiles[t])

    def unfolded(tiles):
        if not fold:
            return tiles
        last = rolled(tiles[0], 1 - slots, 0)
        for t in range(1, base):
            last = jnp.where(row % slots == t, rolled(tiles[t], t + 1 - slots, 0), last)
        return tiles + [last]

    def attend():
        drifts = [packed(column) for column in drift]
        factor = packed(inverse)

        def summed(place, h):
            total = None
            for k in range(ngx):
                tile = qr_v[k * spots + place, h].astype(F32)
                gain = jnp.where(above, tile[slots - 1 : slots, :], tile[rp - 1 : rp, :])
                tile = tile + drifts[k] * gain
                total = tile if total is None else total + tile
            return total * factor

        arrived(qr_v.at[pl.ds(0, ngx * spots - 1)], recv_sem.at[0])
        kv_tiles = [summed(place, heads_dev) for place in range(spots)]
        keyval = jnp.concatenate(kv_tiles, 1)
        a = keyval[:, :middle]
        b = keyval[:, middle:HEAD_DIM]
        newkv = jnp.concatenate(
            [a * cosine - b * sine, a * sine + b * cosine, keyval[:, HEAD_DIM:]], 1
        ).astype(BF16)
        newkv_ref[...] = newkv[:seq_dev]
        newkv = newkv.astype(F32)
        owns = []
        for p in range(pairs):
            place, h = 2 * p // heads_dev, 2 * p % heads_dev
            even = summed(place, h).astype(BF16).astype(F32)
            odd = summed(place, h + 1).astype(BF16).astype(F32)
            a = jnp.where(above, even, rolled(odd, slots, 0))
            b = jnp.where(above, rolled(even, slots, 0), odd)
            first = (a * cosine - b * sine).astype(BF16).astype(F32)
            second = (a * sine + b * cosine).astype(BF16).astype(F32)
            rot_v[p, :, :middle] = first
            rot_v[p, :, middle:] = second
            product = first * newkv[:, :middle] + second * newkv[:, middle:HEAD_DIM]
            owns.append(jnp.sum(product, 1, keepdims=True) * scale)
        count = pairs * rp
        rotated = rot_v[...].reshape(count, HEAD_DIM).astype(BF16)
        own = jnp.where(me_owner == 0, jnp.concatenate(owns, 0), masked_fill)
        line = lax.rem(lax.broadcasted_iota(jnp.int32, (count, ctx_dev), 0), slots)
        position = me_owner * ctx_dev + lax.broadcasted_iota(jnp.int32, (count, ctx_dev), 1)
        scores = jnp.full((count, ctx_dev), masked_fill, F32)
        limit = jnp.zeros((count, ctx_dev), jnp.int32)
        loads[5].wait()
        for s in range(seq_dev):
            raw = lax.dot_general(
                rotated,
                cache_v[s, :, :HEAD_DIM],
                (((1,), (1,)), ((), ())),
                preferred_element_type=F32,
            )
            limit = jnp.where(line == s, lengths_ref[s], limit)
            scores = jnp.where(line == s, raw * scale, scores)
        live = position < limit
        scores = jnp.where(live, scores, masked_fill)
        top = jnp.maximum(jnp.max(scores, 1, keepdims=True), own)
        weights = jnp.where(live, jnp.exp(scores - top), 0.0)
        own_weight = jnp.where(me_owner == 0, jnp.exp(own - top), 0.0)
        denom = jnp.sum(weights, 1, keepdims=True) + own_weight
        value = newkv[:, HEAD_DIM:]
        numer = own_weight * jnp.concatenate([value] * pairs, 0)
        for s in range(seq_dev):
            numer = numer + jnp.dot(
                jnp.where(line == s, weights, 0.0).astype(BF16),
                cache_v[s, :, HEAD_DIM:],
                preferred_element_type=F32,
            )
        for d in range(spots):
            side = jnp.zeros((rp, 128), F32)
            tiles = []
            for j in range(pairs_dev):
                low = (d * pairs_dev + j) * rp
                for c in range(HEAD_DIM // 128):
                    tiles.append(numer[low : low + rp, c * 128 : (c + 1) * 128])
                inner = lane % 32
                side = jnp.where((inner >= j * wide) & (inner < 16), top[low : low + rp], side)
                side = jnp.where(inner >= 16 + j * wide, denom[low : low + rp], side)
            for t in range(base):
                part_v[d, t] = folded(tiles, t).astype(BF16)
            part_v[d, base] = split_three(side).astype(BF16)
        mine = gy * owners + me_owner
        for offset in offsets:
            px, py, pz = shifted(*offset)
            send(
                part_v.at[py * ngz + pz],
                prs_v.at[mine],
                send_sem.at[3],
                recv_sem.at[3],
                at(px, py, pz),
            )
        prs_v[mine] = part_v[spot]

    def combine_parts():
        arrived(prs_v.at[pl.ds(0, ngy * owners - 1)], recv_sem.at[3])
        groups = []
        for y in range(ngy):
            sides = []
            for o in range(owners):
                k = y * owners + o
                sides.append(join_three(prs_v[k, base]))
            top = functools.reduce(jnp.maximum, sides)
            factors = [jnp.where(lane < 16, jnp.exp(side - top), 0.0) for side in sides]
            denom = functools.reduce(
                jnp.add, [rolled(f, 16, 1) * side for f, side in zip(factors, sides)]
            )
            share = rolled(1.0 / denom, -16, 1)
            factors = [f * share for f in factors]
            tiles = [None] * (base + fold)
            for o in range(owners):
                pieces = unfolded([prs_v[y * owners + o, t].astype(F32) for t in range(base)])
                for j in range(pairs_dev):
                    f = factors[o][:, j * wide : j * wide + 1]
                    for c in range(HEAD_DIM // 128):
                        t = j * (HEAD_DIM // 128) + c
                        piece = f * pieces[t]
                        tiles[t] = piece if tiles[t] is None else tiles[t] + piece
            groups.append(tiles)
        for h in range(heads_dev):
            for c in range(HEAD_DIM // 128):
                total = jnp.zeros((rp, 128), F32)
                for y in range(ngy):
                    tile = groups[y][(h // 2) * (HEAD_DIM // 128) + c]
                    moved = rolled(tile, y * seq_dev - (h % 2) * slots, 0)
                    inside = (row >= y * seq_dev) & (row < (y + 1) * seq_dev)
                    total = jnp.where(inside, moved, total)
                low = h * HEAD_DIM + c * 128
                heads_v[:, low : low + 128] = total.astype(BF16)

    def hidden():
        arrived(grs_v.at[pl.ds(0, ngx - 1)], recv_sem.at[1])
        g = own_v[0]
        u = own_v[1]
        mean_drift = jnp.zeros((rp, 1), F32)
        for k in range(ngx):
            mean_drift = jnp.where(gx == k, drift[k], mean_drift)
        g = g + mean_drift * g[rows : rows + 1, :]
        u = u + mean_drift * u[rows : rows + 1, :]
        for j in range(ngx - 1):
            peer = other(j)
            shift = jnp.where(gx <= j, drift[j + 1], drift[j])
            g_part = grs_v[peer, 0].astype(F32)
            u_part = grs_v[peer, 1].astype(F32)
            g = g + g_part + shift * g_part[rows : rows + 1, :]
            u = u + u_part + shift * u_part[rows : rows + 1, :]
        g = g * inverse
        u = u * inverse
        hid_v[gx] = (g / (1.0 + jnp.exp(-g)) * u).astype(BF16)
        for j in range(ngx - 1):
            send(hid_v.at[gx], hid_v.at[gx], send_sem.at[4], h_recv.at[gx], at(other(j), gy, gz))

    def down_product(step):
        source = source_at(step)
        if step:
            arrived(hid_v.at[source], h_recv.at[source])
        down_copy(step).wait()
        product = jnp.dot(hid_v[source], down_v[step], preferred_element_type=F32)
        if step:
            acc_v[...] += product
        else:
            acc_v[...] = product

    peers = [o for o in itertools.product(range(ngy), range(ngz)) if any(o)]

    def scoped(name, f, *args):
        with jax.named_scope(name):
            return f(*args)

    scoped("gu0", gate_up, 0)
    for step in range(1, ngx - 1):
        scoped("gu%d" % step, gate_up, step)
    drift, inverse = scoped("moments", moments)
    scoped("attend", attend)
    scoped("gulast", gate_up, ngx - 1)
    scoped("hidden", hidden)
    scoped("down0", down_product, 0)
    scoped("combine", combine_parts)

    def out_product():
        out_copy.wait()
        acc_v[...] += jnp.dot(heads_v[...], out_v[...], preferred_element_type=F32)

    scoped("outp", out_product)
    for step in range(1, ngx - 1):
        scoped("down%d" % step, down_product, step)

    def last_down():
        source = source_at(ngx - 1)
        arrived(hid_v.at[source], h_recv.at[source])
        for part in range(parts):
            columns = slice(part * piece_cols, (part + 1) * piece_cols)
            last_copy(part).wait()
            total = acc_v[:, columns] + jnp.dot(
                hid_v[source], down_v[ngx - 1, :, columns], preferred_element_type=F32
            )
            fin_v[part, spot] = total.astype(BF16)
            for oy, oz in peers:
                px, py, pz = shifted(0, oy, oz)
                send(
                    fin_v.at[part, spot],
                    fin_v.at[part, spot],
                    send_sem.at[5],
                    f_recv.at[part],
                    at(px, py, pz),
                )
            acc_v[:, columns] = total

    scoped("lastdown", last_down)

    def final():
        for part in range(parts):
            columns = slice(part * piece_cols, (part + 1) * piece_cols)
            total = x_v[:, columns] + acc_v[:, columns]
            arrived(fin_v.at[part, pl.ds(0, spots - 1)], f_recv.at[part])
            for oy, oz in peers:
                px, py, pz = shifted(0, oy, oz)
                total = total + fin_v[part, py * ngz + pz].astype(F32)
            mixed_ref[:, columns] = total[:rows].astype(BF16)

    scoped("final", final)

    def drain():
        left(qr_v.at[pl.ds(0, ngx * spots - 1)], send_sem.at[0])
        left(gsend_v, send_sem.at[1])
        left(stat_v.at[pl.ds(0, ngx - 1)], send_sem.at[2])
        left(prs_v.at[pl.ds(0, ngy * owners - 1)], send_sem.at[3])
        left(hid_v.at[pl.ds(0, ngx - 1)], send_sem.at[4])
        left(fin_v.at[:, pl.ds(0, spots - 1)], send_sem.at[5])

    scoped("drain", drain)


def write_out(mixed_v, newkv_v, mixed_h, newkv_h, sem):
    first = pltpu.make_async_copy(mixed_v, mixed_h, sem.at[0])
    second = pltpu.make_async_copy(newkv_v, newkv_h, sem.at[1])
    first.start()
    second.start()
    first.wait()
    second.wait()


def fused(sizes, *args):
    (tokens, gain, qw, kvw, outw, gatew, upw, downw, cache, lengths) = args
    ngx, ngy, ngz = sizes
    rows, dx = tokens.shape
    rp = (rows // 8 + 1) * 8
    qd = qw.shape[1]
    fb = gatew.shape[1] // ngx
    heads_dev = qd // HEAD_DIM
    owners = ngx * ngz
    spots = ngy * ngz
    kw = kvw.shape[1] // spots
    middle = HEAD_DIM // 2
    slots = rp // 2
    tiles = heads_dev // 2 * (HEAD_DIM // 128)
    fold = tiles == slots and cache.shape[0] == slots - 1
    tiles = tiles - fold + 1
    dma = pltpu.SemaphoreType.DMA
    vm = pltpu.VMEM
    scratch = [
        pltpu.SMEM(lengths.shape, jnp.int32),
        vm(tokens.shape, BF16),
        vm((1, dx), F32),
        vm(qw.shape, BF16),
        vm((dx, kw), BF16),
        vm(cache.shape, BF16),
        vm((ngx, 2, dx, fb), BF16),
        vm(outw.shape, BF16),
        vm((ngx, fb, dx), BF16),
        dma((6,)),
        dma((2, ngx)),
        vm((rp, dx), F32),
        vm((rp, dx), BF16),
        vm((ngx, rp, 128), BF16),
        vm((ngy, heads_dev + 1, rp, 128), BF16),
        vm((ngx * spots, heads_dev + 1, rp, 128), BF16),
        vm((HEADS // 2, rp, HEAD_DIM), F32),
        vm((spots, tiles, rp, 128), BF16),
        vm((ngy * owners, tiles, rp, 128), BF16),
        vm((ngx - 1, 2, rp, fb), BF16),
        vm((ngx, 2, rp, fb), BF16),
        vm((2, rp, fb), F32),
        vm((ngx, rp, fb), BF16),
        vm((rp, dx), F32),
        vm((rp, qd), BF16),
        vm((2, spots, rp, dx // 2), BF16),
        dma((6,)),
        dma((4,)),
        dma((ngx,)),
        dma((2,)),
    ]
    anywhere = pl.BlockSpec(memory_space=pl.ANY)
    results = pl.pallas_call(
        functools.partial(kernel, (ngx, ngy, ngz, rows, rp)),
        out_shape=(
            pltpu.VMEM(tokens.shape, BF16),
            pltpu.VMEM((cache.shape[0], 2 * HEAD_DIM), BF16),
        ),
        in_specs=[anywhere] * 10,
        out_specs=(pl.BlockSpec(memory_space=pltpu.VMEM),) * 2,
        scratch_shapes=scratch,
        compiler_params=pltpu.CompilerParams(
            collective_id=0, has_side_effects=True, vmem_limit_bytes=61 * 2**20
        ),
    )(lengths, tokens, gain.reshape(1, dx), qw, kvw, cache, gatew, upw, outw, downw)
    results = [pltpu.with_memory_space_constraint(a, vm) for a in results]
    return pl.pallas_call(
        write_out,
        out_shape=tuple(pltpu.HBM(a.shape, a.dtype) for a in results),
        in_specs=[pl.BlockSpec(memory_space=vm)] * 2,
        out_specs=(pl.BlockSpec(memory_space=pltpu.HBM),) * 2,
        scratch_shapes=[dma((2,))],
    )(*results)


def fits(sizes, rows, seq_dev, d_dev, q_dev, ff_dev, weight_bytes):
    ngx, ngy, ngz = sizes
    heads_dev = q_dev // HEAD_DIM
    return (
        ngx >= 4
        and ngx & (ngx - 1) == 0
        and rows < 8
        and rows == ngy * seq_dev
        and seq_dev <= 3
        and heads_dev in (2, 4, 8)
        and heads_dev * ngy * ngz == HEADS
        and d_dev % 1024 == 0
        and 2 * HEAD_DIM == ngy * ngz * 128
        and ff_dev % (ngx * 128) == 0
        and weight_bytes <= 60 * 2**20
    )


def choose(sizes, *args):
    held = sum(a.size * a.dtype.itemsize for a in args[2:9])
    rows, d_dev = args[0].shape
    seq_dev = args[8].shape[0]
    if fits(sizes, rows, seq_dev, d_dev, args[2].shape[1], args[5].shape[1], held):
        return fused(sizes, *args)
    return body(*args)


def solution(mesh):
    sizes = tuple(mesh.shape[a] for a in ("gx", "gy", "gz"))
    chosen = functools.partial(choose, sizes)
    in_specs = (
        P("group", "gx"),
        P("gx"),
        P("gx", ("gy", "gz")),
        P("gx", None),
        P(("gy", "gz"), "gx"),
        P("gx", ("gy", "gz")),
        P("gx", ("gy", "gz")),
        P(("gy", "gz"), "gx"),
        P(("group", "gy"), ("gx", "gz"), None),
        P(("group", "gy")),
    )
    out_specs = (P("group", "gx"), P(("group", "gy"), None))
    return jax.shard_map(chosen, mesh=mesh, in_specs=in_specs, out_specs=out_specs, check_vma=False)
```

```python
import functools
import itertools

import jax
import jax.numpy as jnp
import numpy as np
from jax import lax
from jax.experimental import pallas as pl
from jax.experimental.pallas import tpu as pltpu
from jax.sharding import PartitionSpec as P

D = 8192
HEADS = 16
HEAD_DIM = 256


epsilon = 1e-05
masked_fill = -1e30
rotary_base = 10000.0


def joined(part, axis, combine):
    gathered = jax.tree.map(lambda a: lax.all_gather(a, axis), part)

    def take(source):
        return jax.tree.map(lambda a: lax.dynamic_index_in_dim(a, source, 0, False), gathered)

    return lax.fori_loop(
        1, lax.axis_size(axis), lambda source, state: combine(state, take(source)), take(0)
    )


def rotate(values, angle):
    middle = values.shape[-1] // 2
    first = values[..., :middle]
    second = values[..., middle:]
    cosine = jnp.cos(angle)
    sine_part = jnp.sin(angle)
    return jnp.concatenate(
        [first * cosine - second * sine_part, first * sine_part + second * cosine], -1
    )


def angles(lengths, head_dim):
    middle = head_dim // 2
    spread = rotary_base ** (-jnp.arange(middle, dtype=jnp.float32) / middle)
    return lengths.astype(jnp.float32)[:, None] * spread[None, :]


def combine(earlier, later):
    top = jnp.maximum(earlier[0], later[0])
    first_scale = jnp.exp(earlier[0] - top)
    second_scale = jnp.exp(later[0] - top)
    numer = earlier[1] * first_scale[..., None] + later[1] * second_scale[..., None]
    denom = earlier[2] * first_scale + later[2] * second_scale
    return (top, numer, denom)


def body(
    tokens,
    norm_gain,
    q_weight,
    kv_weight,
    out_weight,
    gate_weight,
    up_weight,
    down_weight,
    kv_cache,
    lengths,
):
    inputs = tokens.astype(jnp.float32)
    totals = lax.psum((jnp.sum(inputs, 1), jnp.sum(inputs * inputs, 1)), "gx")
    center = totals[0] / D
    spread_sq = totals[1] / D - center * center
    normed = (
        (inputs - center[:, None]) * lax.rsqrt(spread_sq + epsilon)[:, None] * norm_gain[None, :]
    ).astype(jnp.bfloat16)
    query_part = jnp.dot(normed, q_weight, preferred_element_type=jnp.float32)
    keyval_part = jnp.dot(normed, kv_weight, preferred_element_type=jnp.float32)
    gate_part = jnp.dot(normed, gate_weight, preferred_element_type=jnp.float32)
    up_part = jnp.dot(normed, up_weight, preferred_element_type=jnp.float32)
    query, keyval, gate, upward = lax.psum((query_part, keyval_part, gate_part, up_part), "gx")
    hidden = (jax.nn.silu(gate) * upward).astype(jnp.bfloat16)
    seq_dev = lengths.shape[0]
    row_groups = lax.axis_size("gy")
    block = q_weight.shape[1]
    first_row = lax.axis_index("gy") * seq_dev
    angle = angles(lengths, HEAD_DIM)
    own_keyval = lax.dynamic_slice_in_dim(keyval, first_row, seq_dev, 0)
    new_kv = jnp.concatenate(
        [rotate(own_keyval[:, :HEAD_DIM], angle), own_keyval[:, HEAD_DIM:]], 1
    ).astype(jnp.bfloat16)
    query_bf = query.astype(jnp.bfloat16)
    every_head = lax.all_gather(query_bf, ("gy", "gz"), axis=1, tiled=True)
    own_query = lax.dynamic_slice_in_dim(every_head, first_row, seq_dev, 0)
    rotated = rotate(
        own_query.astype(jnp.float32).reshape(seq_dev, HEADS, HEAD_DIM), angle[:, None, :]
    ).astype(jnp.bfloat16)
    ctx_dev = kv_cache.shape[1]
    offset = lax.axis_index(("gx", "gz")) * ctx_dev
    positions = offset + jnp.arange(ctx_dev, dtype=jnp.int32)
    live = positions[None, :] < lengths[:, None]
    scale = HEAD_DIM ** (-0.5)
    scores = (
        jnp.einsum(
            "shd,scd->shc", rotated, kv_cache[:, :, :HEAD_DIM], preferred_element_type=jnp.float32
        )
        * scale
    )
    key_new = new_kv[:, :HEAD_DIM]
    value_new = new_kv[:, HEAD_DIM:]
    own_score = (
        jnp.einsum("shd,sd->sh", rotated, key_new, preferred_element_type=jnp.float32) * scale
    )
    hidden_scores = jnp.where(live[:, None, :], scores, masked_fill)
    local_top = jnp.maximum(jnp.max(hidden_scores, 2), own_score)
    weights = jnp.where(live[:, None, :], jnp.exp(hidden_scores - local_top[..., None]), 0.0)
    numer = jnp.einsum(
        "shc,scd->shd",
        weights.astype(jnp.bfloat16),
        kv_cache[:, :, HEAD_DIM:],
        preferred_element_type=jnp.float32,
    )
    denom = jnp.sum(weights, 2)
    top, numer, denom = joined((local_top, numer, denom), ("gx", "gz"), combine)
    own_weight = jnp.exp(own_score - top)
    numer = numer + own_weight[..., None] * value_new.astype(jnp.float32)[:, None, :]
    denom = denom + own_weight
    attended = (numer / denom[..., None]).astype(jnp.bfloat16)
    grouped = attended.reshape(seq_dev, row_groups, HEADS * HEAD_DIM // row_groups)
    picked = lax.dynamic_slice_in_dim(grouped, lax.axis_index("gz") * block, block, 2)
    head_block = lax.all_to_all(picked, "gy", split_axis=1, concat_axis=0, tiled=True).reshape(
        seq_dev * row_groups, block
    )
    partial_value = jnp.dot(head_block, out_weight, preferred_element_type=jnp.float32) + jnp.dot(
        hidden, down_weight, preferred_element_type=jnp.float32
    )
    total = lax.psum(partial_value, ("gy", "gz"))
    mixed = (inputs + total).astype(jnp.bfloat16)
    return (mixed, new_kv)


MESH = pl.DeviceIdType.MESH
F32 = jnp.float32
BF16 = jnp.bfloat16


def kernel(
    dims,
    lengths_h,
    tokens_h,
    gain_h,
    q_h,
    kv_h,
    cache_h,
    gate_h,
    up_h,
    out_h,
    down_h,
    mixed_ref,
    newkv_ref,
    lengths_ref,
    tokens_v,
    gain_v,
    q_v,
    kv_v,
    cache_v,
    gu_v,
    out_v,
    down_v,
    load_sem,
    gu_sem,
    x_v,
    normed_v,
    stat_v,
    q1_v,
    qr_v,
    rot_v,
    part_v,
    prs_v,
    gsend_v,
    grs_v,
    own_v,
    hid_v,
    acc_v,
    heads_v,
    fin_v,
    send_sem,
    recv_sem,
    h_recv,
    f_recv,
):
    ngx, ngy, ngz, rows, rp = dims
    gx, gy, gz = lax.axis_index("gx"), lax.axis_index("gy"), lax.axis_index("gz")
    dx = x_v.shape[1]
    qd = q_v.shape[1]
    heads_dev = qd // HEAD_DIM
    kw = kv_v.shape[1]
    seq_dev = cache_v.shape[0]
    ctx_dev = cache_v.shape[1]
    fb = gu_v.shape[3]
    owners = ngx * ngz
    spots = ngy * ngz
    pairs = HEADS // 2
    pairs_dev = heads_dev // 2
    slots = rp // 2
    wide = 16 // pairs_dev
    scale = HEAD_DIM ** (-0.5)
    middle = HEAD_DIM // 2
    parts = fin_v.shape[0]
    piece_cols = dx // parts
    me_owner = gx * ngz + gz
    spot = gy * ngz + gz

    def rolled(values, shift, axis):
        shift = shift % values.shape[axis]
        return pltpu.roll(values, shift, axis) if shift else values

    lane = lax.broadcasted_iota(jnp.int32, (rp, 128), 1)
    row = lax.broadcasted_iota(jnp.int32, (rp, 128), 0)
    above = row < slots

    def split_three(values):
        pieces = []
        for c in range(2):
            scaled = values * 65537.0
            pieces.append(scaled - (scaled - values))
            values = values - pieces[-1]
        return jnp.where(lane < 32, pieces[0], jnp.where(lane < 64, pieces[1], values))

    def join_three(pieces):
        pieces = pieces.astype(F32)
        return pieces + rolled(pieces, -32, 1) + rolled(pieces, -64, 1)

    def other(j):
        return jnp.where(gx <= j, j + 1, j)

    def partner(mask):
        result = gx
        for g in range(ngx):
            result = jnp.where(gx == g, g ^ mask, result)
        return result

    def block_at(step):
        if step == ngx - 1:
            return gx
        return partner(ngx - 1 - step)

    def source_at(step):
        return gx if step == 0 else other(step - 1)

    def columns_of(block, width):
        return pl.ds(pl.multiple_of(block * width, width), width)

    loads = [
        pltpu.make_async_copy(a, b, load_sem.at[i])
        for i, (a, b) in enumerate(
            (
                (tokens_h, tokens_v),
                (gain_h, gain_v),
                (lengths_h, lengths_ref),
                (kv_h.at[:, columns_of(spot, kw)], kv_v),
                (q_h, q_v),
                (cache_h, cache_v),
            )
        )
    ]

    def gu_start(step):
        columns = columns_of(block_at(step), fb)
        pltpu.make_async_copy(gate_h.at[:, columns], gu_v.at[step, 0], gu_sem.at[0, step]).start()
        pltpu.make_async_copy(up_h.at[:, columns], gu_v.at[step, 1], gu_sem.at[1, step]).start()

    def again(k):
        return gu_sem.at[k % 2, k // 2]

    out_copy = pltpu.make_async_copy(out_h, out_v, again(1))

    def down_copy(step):
        picked = columns_of(source_at(step), fb)
        return pltpu.make_async_copy(down_h.at[picked], down_v.at[step], again(step + (step > 0)))

    def last_copy(part):
        picked = columns_of(source_at(ngx - 1), fb)
        columns = pl.ds(part * piece_cols, piece_cols)
        return pltpu.make_async_copy(
            down_h.at[picked, columns],
            down_v.at[ngx - 1, :, columns],
            again(ngx + part),
        )

    offsets = [o for o in itertools.product(range(ngx), range(ngy), range(ngz)) if any(o)]

    def shifted(ox, oy, oz):
        return lax.rem(gx + ox, ngx), lax.rem(gy + oy, ngy), lax.rem(gz + oz, ngz)

    def at(px, py, pz):
        return {"gx": px, "gy": py, "gz": pz}

    for i in range(5):
        loads[i].start()

    barrier = pltpu.get_barrier_semaphore()
    for offset in offsets:
        pl.semaphore_signal(barrier, inc=1, device_id=at(*shifted(*offset)), device_id_type=MESH)

    loads[0].wait()
    gu_start(0)
    x_v[...] = jnp.zeros_like(x_v)
    x_v[0:rows, :] = tokens_v[...].astype(F32)
    x = x_v[...]
    sums = jnp.sum(x, 1, keepdims=True)
    stat = jnp.where(lane % 32 < 16, sums, jnp.sum(x * x, 1, keepdims=True))
    stat = split_three(stat).astype(BF16)
    loads[1].wait()
    gu_start(1)
    spare = lax.broadcasted_iota(jnp.int32, (rp, dx), 0) == rows
    centred = jnp.where(spare, 1.0, x - sums / dx)
    normed_v[...] = (centred * gain_v[...]).astype(BF16)

    loads[2].wait()
    loads[5].start()
    line = lax.rem(lax.broadcasted_iota(jnp.int32, (rp, middle), 0), slots)
    length = jnp.zeros((rp, middle), jnp.int32)
    for s in range(seq_dev):
        length = jnp.where(line == s, lengths_ref[s], length)
    place = lax.broadcasted_iota(jnp.int32, (rp, middle), 1).astype(F32)
    angle = length.astype(F32) * jnp.exp(place * (-np.log(rotary_base) / middle))
    cosine = jnp.cos(angle)
    sine = jnp.sin(angle)

    loads[3].wait()
    gu_start(2)
    kv_part = jnp.dot(normed_v[...], kv_v[...], preferred_element_type=F32)
    loads[4].wait()
    for step in range(3, ngx):
        gu_start(step)
    q_part = jnp.dot(normed_v[...], q_v[...], preferred_element_type=F32)
    stat_v[gx] = stat
    for y in range(ngy):
        for h in range(heads_dev + 1):
            a = q_part[:, h * HEAD_DIM : h * HEAD_DIM + middle] if h < heads_dev else kv_part
            b = q_part[:, h * HEAD_DIM + middle : (h + 1) * HEAD_DIM] if h < heads_dev else a
            tile = jnp.where(above, rolled(a, -y * seq_dev, 0), rolled(b, slots - y * seq_dev, 0))
            tile = jnp.where(row == slots - 1, a[rows : rows + 1, :], tile)
            tile = jnp.where(row == rp - 1, b[rows : rows + 1, :], tile)
            q1_v[y, h] = tile.astype(BF16)

    pl.semaphore_wait(barrier, len(offsets))

    def send(source, target, sends, receives, device):
        pltpu.make_async_remote_copy(
            src_ref=source,
            dst_ref=target,
            send_sem=sends,
            recv_sem=receives,
            device_id=device,
            device_id_type=MESH,
        ).start()

    def arrival(slot, semaphore):
        return pltpu.make_async_remote_copy(
            src_ref=slot,
            dst_ref=slot,
            send_sem=semaphore,
            recv_sem=semaphore,
            device_id=at(gx, gy, gz),
            device_id_type=MESH,
        )

    def arrived(slot, semaphore):
        arrival(slot, semaphore).wait_recv()

    def left(slot, semaphore):
        arrival(slot, semaphore).wait_send()

    for j in range(ngx - 1):
        peer = at(other(j), gy, gz)
        send(stat_v.at[gx], stat_v.at[gx], send_sem.at[2], recv_sem.at[2], peer)
    for offset in offsets:
        px, py, pz = shifted(*offset)
        send(
            q1_v.at[py],
            qr_v.at[gx * spots + spot],
            send_sem.at[0],
            recv_sem.at[0],
            at(px, py, pz),
        )
    qr_v[gx * spots + spot] = q1_v[gy]

    def later_loads(k):
        if k == 0:
            down_copy(0).start()
        elif k == 1:
            out_copy.start()
        elif k < ngx:
            down_copy(k - 1).start()
        elif k < ngx + parts:
            last_copy(k - ngx).start()

    def gate_up(step):
        for which in range(2):
            slot = gu_v.at[step, which]
            pltpu.make_async_copy(slot, slot, gu_sem.at[which, step]).wait()
            later_loads(2 * step + which)
            part = jnp.dot(normed_v[...], gu_v[step, which], preferred_element_type=F32)
            if step < ngx - 1:
                gsend_v[step, which] = part.astype(BF16)
            else:
                own_v[which] = part
        if step < ngx - 1:
            send(
                gsend_v.at[step],
                grs_v.at[gx],
                send_sem.at[1],
                recv_sem.at[1],
                at(block_at(step), gy, gz),
            )

    def moments():
        arrived(stat_v.at[pl.ds(0, ngx - 1)], recv_sem.at[2])
        stats = [join_three(stat_v[k]) for k in range(ngx)]
        totals = functools.reduce(jnp.add, stats)
        center = totals[:, 0:1] / D
        spread_sq = totals[:, 16:17] / D - center * center
        drift = [part[:, 0:1] / dx - center for part in stats]
        return drift, lax.rsqrt(spread_sq + epsilon)

    def packed(column):
        values = jnp.broadcast_to(column, (rp, 128))
        result = None
        for y in range(ngy):
            upper = rolled(values, -y * seq_dev, 0)
            lower = rolled(values, slots - y * seq_dev, 0)
            choice = jnp.where(above, upper, lower)
            result = choice if result is None else jnp.where(gy == y, choice, result)
        return result

    fold = pairs_dev * (HEAD_DIM // 128) == slots and seq_dev == slots - 1
    base = pairs_dev * (HEAD_DIM // 128) - fold

    def folded(tiles, t):
        if not fold:
            return tiles[t]
        return jnp.where(row % slots == slots - 1, rolled(tiles[-1], slots - 1 - t, 0), tiles[t])

    def unfolded(tiles):
        if not fold:
            return tiles
        last = rolled(tiles[0], 1 - slots, 0)
        for t in range(1, base):
            last = jnp.where(row % slots == t, rolled(tiles[t], t + 1 - slots, 0), last)
        return tiles + [last]

    def attend():
        drifts = [packed(column) for column in drift]
        factor = packed(inverse)

        def summed(place, h):
            total = None
            for k in range(ngx):
                tile = qr_v[k * spots + place, h].astype(F32)
                gain = jnp.where(above, tile[slots - 1 : slots, :], tile[rp - 1 : rp, :])
                tile = tile + drifts[k] * gain
                total = tile if total is None else total + tile
            return total * factor

        arrived(qr_v.at[pl.ds(0, ngx * spots - 1)], recv_sem.at[0])
        kv_tiles = [summed(place, heads_dev) for place in range(spots)]
        keyval = jnp.concatenate(kv_tiles, 1)
        a = keyval[:, :middle]
        b = keyval[:, middle:HEAD_DIM]
        newkv = jnp.concatenate(
            [a * cosine - b * sine, a * sine + b * cosine, keyval[:, HEAD_DIM:]], 1
        ).astype(BF16)
        newkv_ref[...] = newkv[:seq_dev]
        newkv = newkv.astype(F32)
        owns = []
        for p in range(pairs):
            place, h = 2 * p // heads_dev, 2 * p % heads_dev
            even = summed(place, h).astype(BF16).astype(F32)
            odd = summed(place, h + 1).astype(BF16).astype(F32)
            a = jnp.where(above, even, rolled(odd, slots, 0))
            b = jnp.where(above, rolled(even, slots, 0), odd)
            first = (a * cosine - b * sine).astype(BF16).astype(F32)
            second = (a * sine + b * cosine).astype(BF16).astype(F32)
            rot_v[p, :, :middle] = first
            rot_v[p, :, middle:] = second
            product = first * newkv[:, :middle] + second * newkv[:, middle:HEAD_DIM]
            owns.append(jnp.sum(product, 1, keepdims=True) * scale)
        count = pairs * rp
        rotated = rot_v[...].reshape(count, HEAD_DIM).astype(BF16)
        own = jnp.where(me_owner == 0, jnp.concatenate(owns, 0), masked_fill)
        line = lax.rem(lax.broadcasted_iota(jnp.int32, (count, ctx_dev), 0), slots)
        position = me_owner * ctx_dev + lax.broadcasted_iota(jnp.int32, (count, ctx_dev), 1)
        scores = jnp.full((count, ctx_dev), masked_fill, F32)
        limit = jnp.zeros((count, ctx_dev), jnp.int32)
        loads[5].wait()
        for s in range(seq_dev):
            raw = lax.dot_general(
                rotated,
                cache_v[s, :, :HEAD_DIM],
                (((1,), (1,)), ((), ())),
                preferred_element_type=F32,
            )
            limit = jnp.where(line == s, lengths_ref[s], limit)
            scores = jnp.where(line == s, raw * scale, scores)
        live = position < limit
        scores = jnp.where(live, scores, masked_fill)
        top = jnp.maximum(jnp.max(scores, 1, keepdims=True), own)
        weights = jnp.where(live, jnp.exp(scores - top), 0.0)
        own_weight = jnp.where(me_owner == 0, jnp.exp(own - top), 0.0)
        denom = jnp.sum(weights, 1, keepdims=True) + own_weight
        value = newkv[:, HEAD_DIM:]
        numer = own_weight * jnp.concatenate([value] * pairs, 0)
        for s in range(seq_dev):
            numer = numer + jnp.dot(
                jnp.where(line == s, weights, 0.0).astype(BF16),
                cache_v[s, :, HEAD_DIM:],
                preferred_element_type=F32,
            )
        for d in range(spots):
            side = jnp.zeros((rp, 128), F32)
            tiles = []
            for j in range(pairs_dev):
                low = (d * pairs_dev + j) * rp
                for c in range(HEAD_DIM // 128):
                    tiles.append(numer[low : low + rp, c * 128 : (c + 1) * 128])
                inner = lane % 32
                side = jnp.where((inner >= j * wide) & (inner < 16), top[low : low + rp], side)
                side = jnp.where(inner >= 16 + j * wide, denom[low : low + rp], side)
            for t in range(base):
                part_v[d, t] = folded(tiles, t).astype(BF16)
            part_v[d, base] = split_three(side).astype(BF16)
        mine = gy * owners + me_owner
        for offset in offsets:
            px, py, pz = shifted(*offset)
            send(
                part_v.at[py * ngz + pz],
                prs_v.at[mine],
                send_sem.at[3],
                recv_sem.at[3],
                at(px, py, pz),
            )
        prs_v[mine] = part_v[spot]

    def combine_parts():
        arrived(prs_v.at[pl.ds(0, ngy * owners - 1)], recv_sem.at[3])
        groups = []
        for y in range(ngy):
            sides = []
            for o in range(owners):
                k = y * owners + o
                sides.append(join_three(prs_v[k, base]))
            top = functools.reduce(jnp.maximum, sides)
            factors = [jnp.where(lane < 16, jnp.exp(side - top), 0.0) for side in sides]
            denom = functools.reduce(
                jnp.add, [rolled(f, 16, 1) * side for f, side in zip(factors, sides)]
            )
            share = rolled(1.0 / denom, -16, 1)
            factors = [f * share for f in factors]
            tiles = [None] * (base + fold)
            for o in range(owners):
                pieces = unfolded([prs_v[y * owners + o, t].astype(F32) for t in range(base)])
                for j in range(pairs_dev):
                    f = factors[o][:, j * wide : j * wide + 1]
                    for c in range(HEAD_DIM // 128):
                        t = j * (HEAD_DIM // 128) + c
                        piece = f * pieces[t]
                        tiles[t] = piece if tiles[t] is None else tiles[t] + piece
            groups.append(tiles)
        for h in range(heads_dev):
            for c in range(HEAD_DIM // 128):
                total = jnp.zeros((rp, 128), F32)
                for y in range(ngy):
                    tile = groups[y][(h // 2) * (HEAD_DIM // 128) + c]
                    moved = rolled(tile, y * seq_dev - (h % 2) * slots, 0)
                    inside = (row >= y * seq_dev) & (row < (y + 1) * seq_dev)
                    total = jnp.where(inside, moved, total)
                low = h * HEAD_DIM + c * 128
                heads_v[:, low : low + 128] = total.astype(BF16)

    def hidden():
        arrived(grs_v.at[pl.ds(0, ngx - 1)], recv_sem.at[1])
        g = own_v[0]
        u = own_v[1]
        mean_drift = jnp.zeros((rp, 1), F32)
        for k in range(ngx):
            mean_drift = jnp.where(gx == k, drift[k], mean_drift)
        g = g + mean_drift * g[rows : rows + 1, :]
        u = u + mean_drift * u[rows : rows + 1, :]
        for j in range(ngx - 1):
            peer = other(j)
            shift = jnp.where(gx <= j, drift[j + 1], drift[j])
            g_part = grs_v[peer, 0].astype(F32)
            u_part = grs_v[peer, 1].astype(F32)
            g = g + g_part + shift * g_part[rows : rows + 1, :]
            u = u + u_part + shift * u_part[rows : rows + 1, :]
        g = g * inverse
        u = u * inverse
        hid_v[gx] = (g / (1.0 + jnp.exp(-g)) * u).astype(BF16)
        for j in range(ngx - 1):
            send(hid_v.at[gx], hid_v.at[gx], send_sem.at[4], h_recv.at[gx], at(partner(j + 1), gy, gz))

    def down_product(step):
        source = source_at(step)
        if step:
            arrived(hid_v.at[source], h_recv.at[source])
        down_copy(step).wait()
        product = jnp.dot(hid_v[source], down_v[step], preferred_element_type=F32)
        if step:
            acc_v[...] += product
        else:
            acc_v[...] = product

    peers = sorted(
        (o for o in itertools.product(range(ngy), range(ngz)) if any(o)),
        key=lambda o: (-o[0], o[1]),
    )

    def scoped(name, f, *args):
        with jax.named_scope(name):
            return f(*args)

    scoped("gu0", gate_up, 0)
    for step in range(1, ngx - 1):
        scoped("gu%d" % step, gate_up, step)
    drift, inverse = scoped("moments", moments)
    scoped("attend", attend)
    scoped("gulast", gate_up, ngx - 1)
    scoped("hidden", hidden)
    scoped("down0", down_product, 0)
    scoped("down1", down_product, 1)
    scoped("combine", combine_parts)

    def out_product():
        out_copy.wait()
        acc_v[...] += jnp.dot(heads_v[...], out_v[...], preferred_element_type=F32)

    scoped("outp", out_product)
    for step in range(2, ngx - 1):
        scoped("down%d" % step, down_product, step)

    def last_down():
        source = source_at(ngx - 1)
        arrived(hid_v.at[source], h_recv.at[source])
        for part in range(parts):
            columns = slice(part * piece_cols, (part + 1) * piece_cols)
            last_copy(part).wait()
            total = acc_v[:, columns] + jnp.dot(
                hid_v[source], down_v[ngx - 1, :, columns], preferred_element_type=F32
            )
            fin_v[part, spot] = total.astype(BF16)
            for oy, oz in peers:
                px, py, pz = shifted(0, oy, oz)
                send(
                    fin_v.at[part, spot],
                    fin_v.at[part, spot],
                    send_sem.at[5],
                    f_recv.at[part],
                    at(px, py, pz),
                )
            acc_v[:, columns] = total

    scoped("lastdown", last_down)

    def final():
        for part in range(parts):
            columns = slice(part * piece_cols, (part + 1) * piece_cols)
            total = x_v[:, columns] + acc_v[:, columns]
            arrived(fin_v.at[part, pl.ds(0, spots - 1)], f_recv.at[part])
            for oy, oz in peers:
                px, py, pz = shifted(0, oy, oz)
                total = total + fin_v[part, py * ngz + pz].astype(F32)
            mixed_ref[:, columns] = total[:rows].astype(BF16)

    scoped("final", final)

    def drain():
        left(qr_v.at[pl.ds(0, ngx * spots - 1)], send_sem.at[0])
        left(gsend_v, send_sem.at[1])
        left(stat_v.at[pl.ds(0, ngx - 1)], send_sem.at[2])
        left(prs_v.at[pl.ds(0, ngy * owners - 1)], send_sem.at[3])
        left(hid_v.at[pl.ds(0, ngx - 1)], send_sem.at[4])
        left(fin_v.at[:, pl.ds(0, spots - 1)], send_sem.at[5])

    scoped("drain", drain)


def write_out(mixed_v, newkv_v, mixed_h, newkv_h, sem):
    first = pltpu.make_async_copy(mixed_v, mixed_h, sem.at[0])
    second = pltpu.make_async_copy(newkv_v, newkv_h, sem.at[1])
    first.start()
    second.start()
    first.wait()
    second.wait()


def fused(sizes, *args):
    (tokens, gain, qw, kvw, outw, gatew, upw, downw, cache, lengths) = args
    ngx, ngy, ngz = sizes
    rows, dx = tokens.shape
    rp = (rows // 8 + 1) * 8
    qd = qw.shape[1]
    fb = gatew.shape[1] // ngx
    heads_dev = qd // HEAD_DIM
    owners = ngx * ngz
    spots = ngy * ngz
    kw = kvw.shape[1] // spots
    middle = HEAD_DIM // 2
    slots = rp // 2
    tiles = heads_dev // 2 * (HEAD_DIM // 128)
    fold = tiles == slots and cache.shape[0] == slots - 1
    tiles = tiles - fold + 1
    dma = pltpu.SemaphoreType.DMA
    vm = pltpu.VMEM
    scratch = [
        pltpu.SMEM(lengths.shape, jnp.int32),
        vm(tokens.shape, BF16),
        vm((1, dx), F32),
        vm(qw.shape, BF16),
        vm((dx, kw), BF16),
        vm(cache.shape, BF16),
        vm((ngx, 2, dx, fb), BF16),
        vm(outw.shape, BF16),
        vm((ngx, fb, dx), BF16),
        dma((6,)),
        dma((2, ngx)),
        vm((rp, dx), F32),
        vm((rp, dx), BF16),
        vm((ngx, rp, 128), BF16),
        vm((ngy, heads_dev + 1, rp, 128), BF16),
        vm((ngx * spots, heads_dev + 1, rp, 128), BF16),
        vm((HEADS // 2, rp, HEAD_DIM), F32),
        vm((spots, tiles, rp, 128), BF16),
        vm((ngy * owners, tiles, rp, 128), BF16),
        vm((ngx - 1, 2, rp, fb), BF16),
        vm((ngx, 2, rp, fb), BF16),
        vm((2, rp, fb), F32),
        vm((ngx, rp, fb), BF16),
        vm((rp, dx), F32),
        vm((rp, qd), BF16),
        vm((2, spots, rp, dx // 2), BF16),
        dma((6,)),
        dma((4,)),
        dma((ngx,)),
        dma((2,)),
    ]
    anywhere = pl.BlockSpec(memory_space=pl.ANY)
    results = pl.pallas_call(
        functools.partial(kernel, (ngx, ngy, ngz, rows, rp)),
        out_shape=(
            pltpu.VMEM(tokens.shape, BF16),
            pltpu.VMEM((cache.shape[0], 2 * HEAD_DIM), BF16),
        ),
        in_specs=[anywhere] * 10,
        out_specs=(pl.BlockSpec(memory_space=pltpu.VMEM),) * 2,
        scratch_shapes=scratch,
        compiler_params=pltpu.CompilerParams(
            collective_id=0, has_side_effects=True, vmem_limit_bytes=61 * 2**20
        ),
    )(lengths, tokens, gain.reshape(1, dx), qw, kvw, cache, gatew, upw, outw, downw)
    results = [pltpu.with_memory_space_constraint(a, vm) for a in results]
    return pl.pallas_call(
        write_out,
        out_shape=tuple(pltpu.HBM(a.shape, a.dtype) for a in results),
        in_specs=[pl.BlockSpec(memory_space=vm)] * 2,
        out_specs=(pl.BlockSpec(memory_space=pltpu.HBM),) * 2,
        scratch_shapes=[dma((2,))],
    )(*results)


def fits(sizes, rows, seq_dev, d_dev, q_dev, ff_dev, weight_bytes):
    ngx, ngy, ngz = sizes
    heads_dev = q_dev // HEAD_DIM
    return (
        ngx >= 4
        and ngx & (ngx - 1) == 0
        and rows < 8
        and rows == ngy * seq_dev
        and seq_dev <= 3
        and heads_dev in (2, 4, 8)
        and heads_dev * ngy * ngz == HEADS
        and d_dev % 1024 == 0
        and 2 * HEAD_DIM == ngy * ngz * 128
        and ff_dev % (ngx * 128) == 0
        and weight_bytes <= 60 * 2**20
    )


def choose(sizes, *args):
    held = sum(a.size * a.dtype.itemsize for a in args[2:9])
    rows, d_dev = args[0].shape
    seq_dev = args[8].shape[0]
    if fits(sizes, rows, seq_dev, d_dev, args[2].shape[1], args[5].shape[1], held):
        return fused(sizes, *args)
    return body(*args)


def solution(mesh):
    sizes = tuple(mesh.shape[a] for a in ("gx", "gy", "gz"))
    chosen = functools.partial(choose, sizes)
    in_specs = (
        P("group", "gx"),
        P("gx"),
        P("gx", ("gy", "gz")),
        P("gx", None),
        P(("gy", "gz"), "gx"),
        P("gx", ("gy", "gz")),
        P("gx", ("gy", "gz")),
        P(("gy", "gz"), "gx"),
        P(("group", "gy"), ("gx", "gz"), None),
        P(("group", "gy")),
    )
    out_specs = (P("group", "gx"), P(("group", "gy"), None))
    return jax.shard_map(chosen, mesh=mesh, in_specs=in_specs, out_specs=out_specs, check_vma=False)
```
